128 devices in a mesh: seq: 16 (over z, x), head: 8 (over y, core).
Axes of the slice: x: 4, y: 4, z: 4, core: 2. Of those that a mesh axis runs over, the one named last changes fastest.
Arguments:
- query: bfloat16 [8192, 4096], P(('seq', 'head')), may hold values from -41 to 41
- keys: bfloat16 [262144, 1024], P('seq', 'head'), may hold values from -14 to 14
- values: bfloat16 [262144, 1024], P('seq', 'head'), may hold values from -6 to 6
- out_grad: bfloat16 [8192, 4096], P(('seq', 'head')), may hold values from -6 to 6
- span_pos: int32 [16], P('seq'), may hold values from 1 to 31, as said below
- selected: int32 [16, 4], P('seq'), may hold values from -1 to 510, as said below
Outputs:
- attn_out: bfloat16 [8192, 4096], P(('seq', 'head'))
- query_grad: bfloat16 [8192, 4096], P(('seq', 'head'))
- key_grad: bfloat16 [262144, 1024], P('seq', 'head')
- value_grad: bfloat16 [262144, 1024], P('seq', 'head')
The draws below stay inside these ranges and needn't reach their ends.
Inputs may be any that keep to these rules, and one draw needn't show every extreme that they name: `span_pos`: block index of the span's queries within its shard. `selected`: entry [s, j] is -1 if s < j; otherwise it indexes a block of shard s - j (blocks (s - j) * 32 onward), and for j = 0 one earlier than span s's own block s * 32 + span_pos[s].
All inputs are finite; a program needn't handle non-finite values.
Results may differ from the reference program's by a relative error of at most 0.029.
Values may be sent and summed in bfloat16 or wider, within the bound.
A program may use at most 128 MiB of HBM per device.

```python
import jax
import jax.numpy as jnp
from jax import lax

HEADS = 32
KV_HEADS = 8
HEAD_DIM = 128
BLOCK = 512
TOPK = 4
SHARD = 16384
SEQ = 262144
QROWS = 8192
N_SEQ = 16


def pick_blocks(key):
    base_key = jax.random.fold_in(key, 7)
    pos_key, block_key = jax.random.split(base_key, 2)
    shard_blocks = SHARD // BLOCK
    span_block = jax.random.randint(pos_key, (N_SEQ,), 1, shard_blocks)
    device_ids = jnp.arange(N_SEQ)
    pick_ids = jnp.arange(TOPK)
    source = device_ids[:, None] - pick_ids[None, :]
    upper_limit = jnp.where(pick_ids[None, :] == 0, span_block[:, None], shard_blocks)
    within = jax.random.randint(block_key, (N_SEQ, TOPK), 0, 1 << 20) % upper_limit
    chosen = jnp.where(source >= 0, source * shard_blocks + within, -1)
    return (span_block.astype(jnp.int32), chosen.astype(jnp.int32))


def draw_span_pos(key, part):
    return pick_blocks(key)[0]


def draw_selected(key, part):
    return pick_blocks(key)[1]


def draw_keys(key, part):
    key_table = jnp.clip(jax.random.normal(jax.random.fold_in(key, 11), (N_SEQ * SHARD, KV_HEADS * HEAD_DIM), jnp.float32), -4.5, 4.5)
    return key_table.astype(jnp.bfloat16)


def draw_query(key, part):
    query_table = jnp.clip(jax.random.normal(jax.random.fold_in(key, 13), (N_SEQ * BLOCK, HEADS * HEAD_DIM), jnp.float32), -4.5, 4.5)
    return query_table.astype(jnp.bfloat16)


def shard_levels(rng, dims, cuts, least, high):
    def one(dim, blocks):
        draws = jax.random.uniform(jax.random.fold_in(jax.random.fold_in(rng, 6), dim), (blocks,), jnp.float32, least / len(cuts), high / len(cuts))
        return jnp.repeat(jnp.exp(draws), dims[dim] // blocks).reshape((-1,) + (1,) * (len(dims) - dim - 1))

    gain = one(*cuts[0])
    for cut in cuts[1:]:
        gain = gain * one(*cut)
    return gain


def centred(stream_key, dims, width, limit, cuts=(), kind=jnp.bfloat16):
    level = shard_levels(stream_key, dims, cuts, -0.22, 0.18) if cuts else 1.0
    result = jax.random.normal(stream_key, dims, jnp.float32) * width * level
    return jnp.minimum(jnp.maximum(result, -limit), limit).astype(kind)


def setup_inputs(seed: int = 0) -> dict:
    seeds = jax.random.split(jax.random.key(seed), 7)
    return {
        "query": draw_query(jax.random.fold_in(seeds[6], 71), 0),
        "keys": draw_keys(jax.random.fold_in(seeds[6], 71), 0),
        "values": centred(seeds[2], (SEQ, KV_HEADS * HEAD_DIM), 1.0, 6.0, ((0, 16), (1, 8))),
        "out_grad": centred(seeds[3], (QROWS, HEADS * HEAD_DIM), 1.0, 6.0, ((0, 128),)),
        "span_pos": draw_span_pos(jax.random.fold_in(seeds[6], 71), 0),
        "selected": draw_selected(jax.random.fold_in(seeds[6], 71), 0),
    }


masked_score = -1e30


def attend(query_rows, grad_rows, key_rows, value_rows, allowed, score_scale):
    query_float = query_rows.astype(jnp.float32)
    grad_float = grad_rows.astype(jnp.float32)
    key_float = key_rows.astype(jnp.float32)
    value_float = value_rows.astype(jnp.float32)
    scores = jnp.einsum("qhgd,khd->hgqk", query_float, key_float) * score_scale
    scores = jnp.where(allowed, scores, masked_score)
    row_max = jnp.max(scores, axis=-1, keepdims=True)
    exponent = jnp.exp(scores - row_max)
    weights = exponent / jnp.sum(exponent, axis=-1, keepdims=True)
    weights_low = weights.astype(jnp.bfloat16)
    weights_back = weights_low.astype(jnp.float32)
    attended = jnp.einsum("hgqk,khd->qhgd", weights_back, value_float).astype(jnp.bfloat16)
    row_delta = jnp.sum(grad_float * attended.astype(jnp.float32), axis=-1)
    weight_grad = jnp.einsum("qhgd,khd->hgqk", grad_float, value_float)
    score_grad = (weights * (weight_grad - jnp.transpose(row_delta, (1, 2, 0))[..., None])).astype(jnp.bfloat16)
    grad_back = score_grad.astype(jnp.float32)
    query_part = (jnp.einsum("hgqk,khd->qhgd", grad_back, key_float) * score_scale).astype(jnp.bfloat16)
    key_part = (jnp.einsum("hgqk,qhgd->khd", grad_back, query_float) * score_scale).astype(jnp.bfloat16)
    value_part = jnp.einsum("hgqk,qhgd->khd", weights_back, grad_float).astype(jnp.bfloat16)
    return attended, query_part, key_part, value_part


def reference(query, keys, values, out_grad, span_pos, selected):
    group_size = HEADS // KV_HEADS
    shard_blocks = SHARD // BLOCK
    feature_width = KV_HEADS * HEAD_DIM
    score_scale = HEAD_DIM ** -0.5
    key_total = jnp.zeros(keys.shape, jnp.float32)
    value_total = jnp.zeros(values.shape, jnp.float32)
    columns = jnp.arange((TOPK + 1) * BLOCK)
    query_pos = jnp.arange(BLOCK)
    slot_of = columns // BLOCK
    attended_all = []
    query_grads = []
    for shard_index in range(N_SEQ):
        chosen = selected[shard_index].astype(jnp.int32)
        usable = chosen >= 0
        own_block = shard_index * shard_blocks + span_pos[shard_index].astype(jnp.int32)
        starts = [jnp.maximum(chosen[pick_index], 0) * BLOCK for pick_index in range(TOPK)] + [own_block * BLOCK]
        key_rows = jnp.concatenate([lax.dynamic_slice_in_dim(keys, block_start, BLOCK, 0) for block_start in starts], 0)
        value_rows = jnp.concatenate([lax.dynamic_slice_in_dim(values, block_start, BLOCK, 0) for block_start in starts], 0)
        slot_ok = jnp.concatenate([usable, jnp.ones((1,), jnp.bool_)])[slot_of]
        allowed = jnp.where(slot_of[None, :] == TOPK, (columns % BLOCK)[None, :] <= query_pos[:, None], slot_ok[None, :])
        query_rows = query[shard_index * BLOCK:(shard_index + 1) * BLOCK].reshape(BLOCK, KV_HEADS, group_size, HEAD_DIM)
        grad_rows = out_grad[shard_index * BLOCK:(shard_index + 1) * BLOCK].reshape(BLOCK, KV_HEADS, group_size, HEAD_DIM)
        attended, query_part, key_part, value_part = attend(
            query_rows, grad_rows,
            key_rows.reshape(-1, KV_HEADS, HEAD_DIM), value_rows.reshape(-1, KV_HEADS, HEAD_DIM),
            allowed, score_scale)
        key_part = key_part.reshape(-1, feature_width).astype(jnp.float32)
        value_part = value_part.reshape(-1, feature_width).astype(jnp.float32)
        for pick_index, block_start in enumerate(starts):
            keep_piece = usable[pick_index] if pick_index < TOPK else jnp.ones((), jnp.bool_)
            key_piece = jnp.where(keep_piece, key_part[pick_index * BLOCK:(pick_index + 1) * BLOCK], 0.0)
            value_piece = jnp.where(keep_piece, value_part[pick_index * BLOCK:(pick_index + 1) * BLOCK], 0.0)
            key_total = lax.dynamic_update_slice_in_dim(
                key_total, lax.dynamic_slice_in_dim(key_total, block_start, BLOCK, 0) + key_piece, block_start, 0)
            value_total = lax.dynamic_update_slice_in_dim(
                value_total, lax.dynamic_slice_in_dim(value_total, block_start, BLOCK, 0) + value_piece, block_start, 0)
        attended_all.append(attended.reshape(BLOCK, HEADS * HEAD_DIM))
        query_grads.append(query_part.reshape(BLOCK, HEADS * HEAD_DIM))
    return (jnp.concatenate(attended_all, 0), jnp.concatenate(query_grads, 0),
            key_total.astype(jnp.bfloat16), value_total.astype(jnp.bfloat16))
```

```python
import functools

import jax
import jax.numpy as jnp
from jax import lax
from jax.experimental import pallas as pl
from jax.experimental.pallas import tpu as pltpu
from jax.sharding import PartitionSpec as P

HEAD_DIM = 128
BLOCK = 512
PICKS = 4
SLOTS = PICKS + 1
SCALE = HEAD_DIM ** -0.5
EXP2_SCALE = SCALE * 1.4426950408889634
MASKED = -1e30
MESH = pl.DeviceIdType.MESH
F32 = jnp.float32
BF16 = jnp.bfloat16


def matmul(left, right):
    return jnp.dot(left, right, preferred_element_type=F32)


def attend_kernel(
    seq_count, head_count, groups, shard_blocks,
    sel_ref, pos_ref, q_hbm, og_hbm, k_hbm, v_hbm,
    contrib, attn_recv, qgrad_recv, target_ref,
    sel_recv, k_all, v_all, q_in, og_in, q_heads, og_heads, q_t, og_t,
    key_slots, value_slots, key_t, value_t, kv_send, grad_send, expo,
    max_hist, max_run, sum_run, delta, out_acc, qgrad_acc, kgrad_acc, vgrad_acc, attn_send, qgrad_send,
    load_sem, sel_send_sem, sel_recv_sem, q_send_sem, q_recv_sem, og_send_sem, og_recv_sem,
    kv_send_sem, kv_recv_sem, grad_send_sem, grad_recv_sem, attn_send_sem, attn_recv_sem,
    qgrad_send_sem, qgrad_recv_sem, place_sem,
):
    s = lax.axis_index("seq")
    h = lax.axis_index("head")
    width = groups * HEAD_DIM
    rows = q_hbm.shape[0]

    def columns(index):
        return pl.ds(pl.multiple_of(index * width, width), width)

    def token_rows(index):
        return pl.ds(pl.multiple_of(index * rows, rows), rows)

    load_k = pltpu.make_async_copy(k_hbm, k_all, load_sem.at[0])
    load_v = pltpu.make_async_copy(v_hbm, v_all, load_sem.at[1])
    load_q = pltpu.make_async_copy(q_hbm.at[:, columns(h)], q_in.at[token_rows(h), :], load_sem.at[2])
    load_og = pltpu.make_async_copy(og_hbm.at[:, columns(h)], og_in.at[token_rows(h), :], load_sem.at[3])
    load_k.start()
    load_v.start()
    load_q.start()
    load_og.start()

    barrier = pltpu.get_barrier_semaphore()
    for step in range(1, head_count):
        peer = lax.rem(h + step, head_count)
        pl.semaphore_signal(barrier, inc=1, device_id=(s, peer), device_id_type=MESH)
    for distance in range(1, PICKS):
        for other in (lax.rem(s + distance, seq_count), lax.rem(s + seq_count - distance, seq_count)):
            pl.semaphore_signal(barrier, inc=1, device_id=(other, h), device_id_type=MESH)
    pl.semaphore_wait(barrier, head_count - 1 + 2 * (PICKS - 1))

    def sel_copy(distance):
        return pltpu.make_async_remote_copy(
            src_ref=sel_ref, dst_ref=sel_recv.at[distance - 1],
            send_sem=sel_send_sem.at[distance - 1], recv_sem=sel_recv_sem.at[distance - 1],
            device_id=(s - distance, h), device_id_type=MESH)

    for distance in range(1, PICKS):
        @pl.when(s >= distance)
        def _():
            sel_copy(distance).start()

    def token_copy(source, target, send_sem, recv_sem, step):
        peer = lax.rem(h + step, head_count)
        return pltpu.make_async_remote_copy(
            src_ref=source.at[:, columns(peer)], dst_ref=target.at[token_rows(h), :],
            send_sem=send_sem.at[step], recv_sem=recv_sem.at[step],
            device_id=(s, peer), device_id_type=MESH)

    for step in range(1, head_count):
        token_copy(q_hbm, q_in, q_send_sem, q_recv_sem, step).start()
    for step in range(1, head_count):
        token_copy(og_hbm, og_in, og_send_sem, og_recv_sem, step).start()

    load_k.wait()
    load_v.wait()

    def kv_copy(distance, kind):
        slots = (key_slots, value_slots)[kind]
        return pltpu.make_async_remote_copy(
            src_ref=kv_send.at[distance - 1, kind], dst_ref=slots.at[distance + 1],
            send_sem=kv_send_sem.at[distance - 1, kind], recv_sem=kv_recv_sem.at[distance - 1, kind],
            device_id=(s + distance, h), device_id_type=MESH)

    for distance in range(1, PICKS):
        target_ref[distance + 1] = jnp.int32(-1)

        @pl.when(s + distance < seq_count)
        def _():
            sel_copy(distance).wait_recv()
            entry = lax.rem(sel_recv[distance - 1, 0, distance], shard_blocks)
            target_ref[distance + 1] = entry
            kv_send[distance - 1, 0] = k_all[entry]
            kv_copy(distance, 0).start()
            kv_send[distance - 1, 1] = v_all[entry]
            kv_copy(distance, 1).start()

    own_entry = pos_ref[0]
    first_entry = lax.rem(sel_ref[0, 0], shard_blocks)
    target_ref[0] = own_entry
    target_ref[1] = first_entry
    key_slots[0] = k_all[own_entry]
    value_slots[0] = v_all[own_entry]
    key_slots[1] = k_all[first_entry]
    value_slots[1] = v_all[first_entry]

    load_q.wait()
    for step in range(1, head_count):
        token_copy(q_hbm, q_in, q_send_sem, q_recv_sem, step).wait_recv()
    for group in range(groups):
        piece = q_in[:, group * HEAD_DIM:(group + 1) * HEAD_DIM]
        q_heads[group] = piece
        q_t[group] = piece.T

    def transpose_slot(j):
        key_t[j] = key_slots[j].T
        value_t[j] = value_slots[j].T

    def forward_own(group, carry):
        scores = matmul(key_slots[0], q_t[group])
        key_pos = lax.broadcasted_iota(jnp.int32, scores.shape, 0)
        query_pos = lax.broadcasted_iota(jnp.int32, scores.shape, 1)
        scores = jnp.where(key_pos <= query_pos, scores, MASKED)
        new_max = jnp.max(scores, axis=0, keepdims=True)
        exponent = jnp.exp2((scores - new_max) * EXP2_SCALE)
        expo[0, group] = exponent
        max_hist[0, group] = new_max
        max_run[group] = new_max
        sum_run[group] = jnp.sum(exponent, axis=0, keepdims=True)
        out_acc[group] = matmul(value_t[0], exponent.astype(BF16))
        return carry

    transpose_slot(0)
    lax.fori_loop(0, groups, forward_own, 0)

    def forward_slot(j, carry):
        def forward_group(group, inner):
            scores = matmul(key_slots[j], q_t[group])
            old_max = max_run[group]
            new_max = jnp.maximum(old_max, jnp.max(scores, axis=0, keepdims=True))
            exponent = jnp.exp2((scores - new_max) * EXP2_SCALE)
            expo[j, group] = exponent
            max_hist[j, group] = new_max
            max_run[group] = new_max
            fade = jnp.exp2((old_max - new_max) * EXP2_SCALE)
            sum_run[group] = sum_run[group] * fade + jnp.sum(exponent, axis=0, keepdims=True)
            out_acc[group] = out_acc[group] * fade + matmul(value_t[j], exponent.astype(BF16))
            return inner

        def wait_arrival():
            for kind in range(2):
                pltpu.make_async_remote_copy(
                    src_ref=kv_send.at[j - 2, kind], dst_ref=(key_slots, value_slots)[kind].at[j],
                    send_sem=kv_send_sem.at[j - 2, kind], recv_sem=kv_recv_sem.at[j - 2, kind],
                    device_id=(s, h), device_id_type=MESH).wait_recv()

        @pl.when(s >= j - 1)
        def _():
            pl.when(j >= 2)(wait_arrival)
            transpose_slot(j)
            lax.fori_loop(0, groups, forward_group, 0)
        return carry

    lax.fori_loop(1, SLOTS, forward_slot, 0)

    load_og.wait()
    for step in range(1, head_count):
        token_copy(og_hbm, og_in, og_send_sem, og_recv_sem, step).wait_recv()

    for group in range(groups):
        piece = og_in[:, group * HEAD_DIM:(group + 1) * HEAD_DIM]
        og_heads[group] = piece
        piece_t = piece.T
        og_t[group] = piece_t
        inverse = 1.0 / sum_run[group]
        sum_run[group] = inverse
        attended = (out_acc[group] * inverse).astype(BF16)
        delta[group] = jnp.sum(piece_t.astype(F32) * attended.astype(F32), axis=0, keepdims=True)
        attn_send[:, group * HEAD_DIM:(group + 1) * HEAD_DIM] = attended.T
        qgrad_acc[group] = jnp.zeros_like(qgrad_acc[group])

    def back_copy(source, target, send_sem, recv_sem, step):
        peer = lax.rem(h + step, head_count)
        return pltpu.make_async_remote_copy(
            src_ref=source.at[token_rows(peer), :], dst_ref=target.at[:, columns(h)],
            send_sem=send_sem.at[step], recv_sem=recv_sem.at[step],
            device_id=(s, peer), device_id_type=MESH)

    def back_own(source, target, sem):
        return pltpu.make_async_copy(source.at[token_rows(h), :], target.at[:, columns(h)], sem)

    for step in range(1, head_count):
        back_copy(attn_send, attn_recv, attn_send_sem, attn_recv_sem, step).start()
    back_own(attn_send, attn_recv, place_sem.at[0]).start()

    def grad_copy(j):
        return pltpu.make_async_remote_copy(
            src_ref=grad_send.at[j], dst_ref=contrib.at[j],
            send_sem=grad_send_sem.at[j], recv_sem=grad_recv_sem.at[j],
            device_id=(s - (j - 1), h), device_id_type=MESH)

    def grad_local(j):
        return pltpu.make_async_copy(grad_send.at[j], contrib.at[j], grad_send_sem.at[j])

    def backward_slot(step, carry):
        j = SLOTS - 1 - step

        def backward_group(group, inner):
            factor = jnp.exp2((max_hist[j, group] - max_run[group]) * EXP2_SCALE) * sum_run[group]
            weights = expo[j, group] * factor
            weight_grad = matmul(value_slots[j], og_t[group])
            score_grad = (weights * (weight_grad - delta[group])).astype(BF16)
            vgrad_acc[...] += matmul(weights.astype(BF16), og_heads[group])
            kgrad_acc[...] += matmul(score_grad, q_heads[group])
            qgrad_acc[group] += matmul(key_t[j], score_grad)
            return inner

        @pl.when(s >= j - 1)
        def _():
            vgrad_acc[...] = jnp.zeros_like(vgrad_acc)
            kgrad_acc[...] = jnp.zeros_like(kgrad_acc)
            lax.fori_loop(0, groups, backward_group, 0)
            grad_send[j, 0] = (kgrad_acc[...] * SCALE).astype(BF16)
            grad_send[j, 1] = vgrad_acc[...].astype(BF16)

            @pl.when(j >= 2)
            def _():
                grad_copy(j).start()

            @pl.when(j < 2)
            def _():
                grad_local(j).start()
        return carry

    lax.fori_loop(0, SLOTS, backward_slot, 0)

    for group in range(groups):
        qgrad_send[:, group * HEAD_DIM:(group + 1) * HEAD_DIM] = (qgrad_acc[group] * SCALE).astype(BF16).T
    for step in range(1, head_count):
        back_copy(qgrad_send, qgrad_recv, qgrad_send_sem, qgrad_recv_sem, step).start()
    back_own(qgrad_send, qgrad_recv, place_sem.at[1]).start()

    for step in range(1, head_count):
        token_copy(q_hbm, q_in, q_send_sem, q_recv_sem, step).wait_send()
        token_copy(og_hbm, og_in, og_send_sem, og_recv_sem, step).wait_send()
        back_copy(attn_send, attn_recv, attn_send_sem, attn_recv_sem, step).wait()
    for distance in range(1, PICKS):
        @pl.when(s >= distance)
        def _():
            sel_copy(distance).wait_send()
            grad_copy(distance + 1).wait_send()

        @pl.when(s + distance < seq_count)
        def _():
            kv_copy(distance, 0).wait_send()
            kv_copy(distance, 1).wait_send()
            grad_copy(distance + 1).wait_recv()
    grad_local(0).wait()
    grad_local(1).wait()
    back_own(attn_send, attn_recv, place_sem.at[0]).wait()
    back_own(qgrad_send, qgrad_recv, place_sem.at[1]).wait()
    for step in range(1, head_count):
        back_copy(qgrad_send, qgrad_recv, qgrad_send_sem, qgrad_recv_sem, step).wait()


def place_kernel(
    shard_blocks, target_ref, contrib, attn_in, qgrad_in,
    attn_out, qgrad_out, key_out, value_out,
    zeros, pieces, attn_buf, qgrad_buf, zero_sem, in_sem, out_sem, piece_in_sem, piece_out_sem,
):
    outs = (key_out, value_out)
    attn_load = pltpu.make_async_copy(attn_in, attn_buf, in_sem.at[0])
    qgrad_load = pltpu.make_async_copy(qgrad_in, qgrad_buf, in_sem.at[1])
    attn_load.start()
    qgrad_load.start()

    def piece_load(slot):
        return pltpu.make_async_copy(contrib.at[slot], pieces.at[slot], piece_in_sem.at[slot])

    targets = [target_ref[slot] for slot in range(SLOTS)]
    valid = [target >= 0 for target in targets]
    for slot in range(SLOTS):
        @pl.when(valid[slot])
        def _():
            piece_load(slot).start()

    zeros[...] = jnp.zeros_like(zeros)

    def taken(block):
        hit = targets[0] == block
        for slot in range(1, SLOTS):
            hit = hit | (targets[slot] == block)
        return hit

    def rows_of(block):
        return pl.ds(pl.multiple_of(block * BLOCK, BLOCK), BLOCK)

    def zero_copy(block, kind):
        return pltpu.make_async_copy(zeros, outs[kind].at[rows_of(block), :], zero_sem.at[kind, block])

    def zero_start(block, carry):
        @pl.when(jnp.logical_not(taken(block)))
        def _():
            zero_copy(block, 0).start()
            zero_copy(block, 1).start()
        return carry

    lax.fori_loop(0, shard_blocks, zero_start, 0)

    attn_store = pltpu.make_async_copy(attn_buf, attn_out, out_sem.at[0])
    qgrad_store = pltpu.make_async_copy(qgrad_buf, qgrad_out, out_sem.at[1])
    attn_load.wait()
    attn_store.start()
    qgrad_load.wait()
    qgrad_store.start()

    for slot in range(SLOTS):
        @pl.when(valid[slot])
        def _():
            piece_load(slot).wait()

    leads = []
    for slot in range(SLOTS):
        lead = valid[slot]
        for earlier in range(slot):
            lead = lead & jnp.logical_not(targets[earlier] == targets[slot])
        leads.append(lead)

    def piece_store(slot, kind):
        return pltpu.make_async_copy(
            pieces.at[slot, kind], outs[kind].at[rows_of(targets[slot]), :], piece_out_sem.at[slot, kind])

    for slot in range(SLOTS):
        @pl.when(leads[slot])
        def _():
            repeats = jnp.int32(0)
            for later in range(slot + 1, SLOTS):
                repeats = repeats + jnp.where(targets[later] == targets[slot], 1, 0)

            @pl.when(repeats > 0)
            def _():
                total = pieces[slot].astype(F32)
                for later in range(slot + 1, SLOTS):
                    total = total + jnp.where(targets[later] == targets[slot], pieces[later].astype(F32), 0.0)
                pieces[slot] = total.astype(BF16)
            piece_store(slot, 0).start()
            piece_store(slot, 1).start()

    def zero_wait(block, carry):
        @pl.when(jnp.logical_not(taken(block)))
        def _():
            zero_copy(block, 0).wait()
            zero_copy(block, 1).wait()
        return carry

    lax.fori_loop(0, shard_blocks, zero_wait, 0)
    for slot in range(SLOTS):
        @pl.when(leads[slot])
        def _():
            piece_store(slot, 0).wait()
            piece_store(slot, 1).wait()
    attn_store.wait()
    qgrad_store.wait()


def per_device(query, keys, values, out_grad, span_pos, selected):
    seq_count = lax.axis_size("seq")
    head_count = lax.axis_size("head")
    shard_blocks = keys.shape[0] // BLOCK
    rows, features = query.shape
    width = features // head_count
    groups = width // HEAD_DIM
    any_spec = pl.BlockSpec(memory_space=pl.ANY)
    smem_spec = pl.BlockSpec(memory_space=pltpu.SMEM)
    dma = pltpu.SemaphoreType.DMA
    contrib, attn_recv, qgrad_recv, targets = pl.pallas_call(
        functools.partial(attend_kernel, seq_count, head_count, groups, shard_blocks),
        out_shape=(
            jax.ShapeDtypeStruct((SLOTS, 2, BLOCK, HEAD_DIM), BF16),
            jax.ShapeDtypeStruct(query.shape, BF16),
            jax.ShapeDtypeStruct(query.shape, BF16),
            jax.ShapeDtypeStruct((8,), jnp.int32),
        ),
        in_specs=[smem_spec, smem_spec] + [any_spec] * 4,
        out_specs=(any_spec, any_spec, any_spec, smem_spec),
        scratch_shapes=[
            pltpu.SMEM((PICKS - 1, 1, PICKS), jnp.int32),
            pltpu.VMEM((shard_blocks, BLOCK, HEAD_DIM), BF16),
            pltpu.VMEM((shard_blocks, BLOCK, HEAD_DIM), BF16),
            pltpu.VMEM((BLOCK, width), BF16),
            pltpu.VMEM((BLOCK, width), BF16),
            pltpu.VMEM((groups, BLOCK, HEAD_DIM), BF16),
            pltpu.VMEM((groups, BLOCK, HEAD_DIM), BF16),
            pltpu.VMEM((groups, HEAD_DIM, BLOCK), BF16),
            pltpu.VMEM((groups, HEAD_DIM, BLOCK), BF16),
            pltpu.VMEM((SLOTS, BLOCK, HEAD_DIM), BF16),
            pltpu.VMEM((SLOTS, BLOCK, HEAD_DIM), BF16),
            pltpu.VMEM((SLOTS, HEAD_DIM, BLOCK), BF16),
            pltpu.VMEM((SLOTS, HEAD_DIM, BLOCK), BF16),
            pltpu.VMEM((PICKS - 1, 2, BLOCK, HEAD_DIM), BF16),
            pltpu.VMEM((SLOTS, 2, BLOCK, HEAD_DIM), BF16),
            pltpu.VMEM((SLOTS, groups, BLOCK, BLOCK), F32),
            pltpu.VMEM((SLOTS, groups, 1, BLOCK), F32),
            pltpu.VMEM((groups, 1, BLOCK), F32),
            pltpu.VMEM((groups, 1, BLOCK), F32),
            pltpu.VMEM((groups, 1, BLOCK), F32),
            pltpu.VMEM((groups, HEAD_DIM, BLOCK), F32),
            pltpu.VMEM((groups, HEAD_DIM, BLOCK), F32),
            pltpu.VMEM((BLOCK, HEAD_DIM), F32),
            pltpu.VMEM((BLOCK, HEAD_DIM), F32),
            pltpu.VMEM((BLOCK, width), BF16),
            pltpu.VMEM((BLOCK, width), BF16),
            dma((4,)),
            dma((PICKS - 1,)), dma((PICKS - 1,)),
            dma((head_count,)), dma((head_count,)),
            dma((head_count,)), dma((head_count,)),
            dma((PICKS - 1, 2)), dma((PICKS - 1, 2)),
            dma((SLOTS,)), dma((SLOTS,)),
            dma((head_count,)), dma((head_count,)),
            dma((head_count,)), dma((head_count,)),
            dma((2,)),
        ],
        compiler_params=pltpu.CompilerParams(
            collective_id=0, has_side_effects=True, vmem_limit_bytes=60 * 1024 * 1024),
        name="attend",
    )(selected, span_pos, query, out_grad,
      keys.reshape(shard_blocks, BLOCK, HEAD_DIM), values.reshape(shard_blocks, BLOCK, HEAD_DIM))

    return pl.pallas_call(
        functools.partial(place_kernel, shard_blocks),
        out_shape=(
            jax.ShapeDtypeStruct(query.shape, BF16),
            jax.ShapeDtypeStruct(query.shape, BF16),
            jax.ShapeDtypeStruct(keys.shape, BF16),
            jax.ShapeDtypeStruct(values.shape, BF16),
        ),
        in_specs=[smem_spec, any_spec, any_spec, any_spec],
        out_specs=(any_spec,) * 4,
        scratch_shapes=[
            pltpu.VMEM((BLOCK, HEAD_DIM), BF16),
            pltpu.VMEM((SLOTS, 2, BLOCK, HEAD_DIM), BF16),
            pltpu.VMEM(query.shape, BF16),
            pltpu.VMEM(query.shape, BF16),
            dma((2, shard_blocks)),
            dma((2,)),
            dma((2,)),
            dma((SLOTS,)),
            dma((SLOTS, 2)),
        ],
        name="place",
    )(targets, contrib, attn_recv, qgrad_recv)


def solution(mesh):
    in_specs = (
        P(("seq", "head"), None),
        P("seq", "head"),
        P("seq", "head"),
        P(("seq", "head"), None),
        P("seq"),
        P("seq", None),
    )
    out_specs = (
        P(("seq", "head"), None),
        P(("seq", "head"), None),
        P("seq", "head"),
        P("seq", "head"),
    )
    return jax.shard_map(
        per_device, mesh=mesh, in_specs=in_specs, out_specs=out_specs, check_vma=False
    )
```

```python
import functools

import jax
import jax.numpy as jnp
from jax import lax
from jax.experimental import pallas as pl
from jax.experimental.pallas import tpu as pltpu
from jax.sharding import PartitionSpec as P

HEAD_DIM = 128
BLOCK = 512
PICKS = 4
SLOTS = PICKS + 1
RING = 4
HALVES = 2
SCALE = HEAD_DIM ** -0.5
EXP2_SCALE = SCALE * 1.4426950408889634
MASKED = -1e30
MESH = pl.DeviceIdType.MESH
F32 = jnp.float32
BF16 = jnp.bfloat16


def matmul(left, right):
    return jnp.dot(left, right, preferred_element_type=F32)


def attend_kernel(
    seq_count, head_count, groups, shard_blocks,
    sel_ref, pos_ref, q_hbm, og_hbm, k_hbm, v_hbm,
    contrib, attn_recv, qgrad_recv, target_ref,
    sel_recv, k_all, v_all, q_in, og_in, q_rows, og_rows, q_t, og_t,
    key_slots, value_slots, key_t, value_t, kv_send, grad_send, relay_kv, relay_grad, expo,
    max_hist, max_run, sum_run, delta, out_acc, qgrad_acc, weights_low, scores_low, attn_send, qgrad_send,
    load_sem, sel_send_sem, sel_recv_sem, q_send_sem, q_recv_sem, og_send_sem, og_recv_sem,
    kv_send_sem, kv_recv_sem, relay_send_sem, relay_recv_sem, pass_send_sem,
    grad_send_sem, grad_recv_sem, back_send_sem, back_recv_sem, pass_back_sem,
    attn_send_sem, attn_recv_sem, qgrad_send_sem, qgrad_recv_sem, place_sem,
):
    s = lax.axis_index("seq")
    h = lax.axis_index("head")
    width = groups * HEAD_DIM
    half = width // HALVES
    pair = groups // HALVES
    rows = q_hbm.shape[0]
    column = lax.rem(s, RING)
    relay_out = (column == RING - 1) & (s + 1 < seq_count)
    relay_in = (column == RING - 1) & (s >= RING)
    back_out = (column == 0) & (s >= RING)
    back_in = (column == 0) & (s + RING < seq_count)

    def columns(index):
        return pl.ds(pl.multiple_of(index * width, width), width)

    def half_columns(index, part):
        return pl.ds(pl.multiple_of(index * width + part * half, half), half)

    def token_rows(index):
        return pl.ds(pl.multiple_of(index * rows, rows), rows)

    load_k = pltpu.make_async_copy(k_hbm, k_all, load_sem.at[0])
    load_v = pltpu.make_async_copy(v_hbm, v_all, load_sem.at[1])
    load_q = pltpu.make_async_copy(q_hbm.at[:, columns(h)], q_in.at[token_rows(h), :], load_sem.at[2])
    load_og = pltpu.make_async_copy(og_hbm.at[:, columns(h)], og_in.at[token_rows(h), :], load_sem.at[3])
    load_q.start()
    load_k.start()
    load_v.start()
    load_og.start()

    barrier = pltpu.get_barrier_semaphore()
    for step in range(1, head_count):
        peer = lax.rem(h + step, head_count)
        pl.semaphore_signal(barrier, inc=1, device_id=(s, peer), device_id_type=MESH)
    for distance in range(1, RING + 1):
        for other in (lax.rem(s + distance, seq_count), lax.rem(s + seq_count - distance, seq_count)):
            pl.semaphore_signal(barrier, inc=1, device_id=(other, h), device_id_type=MESH)
    pl.semaphore_wait(barrier, head_count - 1 + 2 * RING)

    def remote(source, target, send_sem, recv_sem, device):
        return pltpu.make_async_remote_copy(
            src_ref=source, dst_ref=target, send_sem=send_sem, recv_sem=recv_sem,
            device_id=device, device_id_type=MESH)

    def sel_copy(distance):
        return remote(
            sel_ref, sel_recv.at[distance - 1], sel_send_sem.at[distance - 1],
            sel_recv_sem.at[distance - 1], (s - distance, h))

    for distance in range(1, PICKS):
        @pl.when(s >= distance)
        def _():
            sel_copy(distance).start()

    def q_copy(step, part):
        peer = lax.rem(h + step, head_count)
        return remote(
            q_hbm.at[:, half_columns(peer, part)], q_in.at[token_rows(h), half_columns(0, part)],
            q_send_sem.at[part, step], q_recv_sem.at[part, step], (s, peer))

    def og_copy(step):
        peer = lax.rem(h + step, head_count)
        return remote(
            og_hbm.at[:, columns(peer)], og_in.at[token_rows(h), :],
            og_send_sem.at[step], og_recv_sem.at[step], (s, peer))

    for part in range(HALVES):
        for step in range(1, head_count):
            q_copy(step, part).start()
    for step in range(1, head_count):
        og_copy(step).start()

    load_k.wait()
    load_v.wait()
    slots = (key_slots, value_slots)

    def kv_copy(distance, kind):
        return remote(
            kv_send.at[distance - 1, kind], slots[kind].at[distance + 1],
            kv_send_sem.at[distance - 1, kind], kv_recv_sem.at[distance - 1, kind], (s + distance, h))

    def relay_copy(kind):
        return remote(
            kv_send.at[0, kind], relay_kv.at[kind], relay_send_sem.at[kind], relay_recv_sem.at[kind],
            (s + RING, h))

    def pass_copy(kind):
        return remote(
            relay_kv.at[kind], slots[kind].at[2], pass_send_sem.at[kind], kv_recv_sem.at[0, kind],
            (s - (RING - 1), h))

    for distance in range(1, PICKS):
        target_ref[distance + 1] = jnp.int32(-1)

        @pl.when(s + distance < seq_count)
        def _():
            sel_copy(distance).wait_recv()
            entry = lax.rem(sel_recv[distance - 1, 0, distance], shard_blocks)
            target_ref[distance + 1] = entry
            for kind in range(2):
                kv_send[distance - 1, kind] = (k_all, v_all)[kind][entry]
                if distance == 1:
                    @pl.when(relay_out)
                    def _():
                        relay_copy(kind).start()

                    @pl.when(jnp.logical_not(relay_out))
                    def _():
                        kv_copy(1, kind).start()
                else:
                    kv_copy(distance, kind).start()

    own_entry = lax.rem(pos_ref[0], shard_blocks)
    first_entry = lax.rem(sel_ref[0, 0], shard_blocks)
    target_ref[0] = own_entry
    target_ref[1] = first_entry

    def transpose_slot(j):
        key_t[j] = key_slots[j].T
        value_t[j] = value_slots[j].T

    for j, entry in enumerate((own_entry, first_entry)):
        key_slots[j] = k_all[entry]
        value_slots[j] = v_all[entry]
        transpose_slot(j)

    def forward_first(group):
        scores = matmul(key_slots[0], q_t[group])
        key_pos = lax.broadcasted_iota(jnp.int32, scores.shape, 0)
        query_pos = lax.broadcasted_iota(jnp.int32, scores.shape, 1)
        scores = jnp.where(key_pos <= query_pos, scores, MASKED)
        new_max = jnp.max(scores, axis=0, keepdims=True)
        exponent = jnp.exp2((scores - new_max) * EXP2_SCALE)
        expo[0, group] = exponent
        max_hist[0, group] = new_max
        max_run[group] = new_max
        sum_run[group] = jnp.sum(exponent, axis=0, keepdims=True)
        out_acc[group] = matmul(value_t[0], exponent.astype(BF16))

    def forward_next(j, group):
        scores = matmul(key_slots[j], q_t[group])
        old_max = max_run[group]
        new_max = jnp.maximum(old_max, jnp.max(scores, axis=0, keepdims=True))
        exponent = jnp.exp2((scores - new_max) * EXP2_SCALE)
        expo[j, group] = exponent
        max_hist[j, group] = new_max
        max_run[group] = new_max
        fade = jnp.exp2((old_max - new_max) * EXP2_SCALE)
        sum_run[group] = sum_run[group] * fade + jnp.sum(exponent, axis=0, keepdims=True)
        out_acc[group] = out_acc[group] * fade + matmul(value_t[j], exponent.astype(BF16))

    load_q.wait()

    def local_part(part, carry):
        for step in range(1, head_count):
            q_copy(step, part).wait_recv()
        for member in range(pair):
            group = part * pair + member
            piece = q_in[:, pl.ds(pl.multiple_of(group * HEAD_DIM, HEAD_DIM), HEAD_DIM)]
            q_rows[pl.ds(pl.multiple_of(group * BLOCK, BLOCK), BLOCK), :] = piece
            q_t[group] = piece.T
        for member in range(pair):
            forward_first(part * pair + member)
        for member in range(pair):
            forward_next(1, part * pair + member)

        @pl.when(relay_in)
        def _():
            for kind in range(2):
                @pl.when(part == kind)
                def _():
                    relay_copy(kind).wait_recv()
                    pass_copy(kind).start()
        return carry

    lax.fori_loop(0, HALVES, local_part, 0)

    def forward_slot(j, carry):
        @pl.when(s >= j - 1)
        def _():
            for kind in range(2):
                remote(
                    kv_send.at[j - 2, kind], slots[kind].at[j], kv_send_sem.at[j - 2, kind],
                    kv_recv_sem.at[j - 2, kind], (s, h)).wait_recv()
            transpose_slot(j)
            for group in range(groups):
                forward_next(j, group)
        return carry

    lax.fori_loop(2, SLOTS, forward_slot, 0)

    load_og.wait()
    for step in range(1, head_count):
        og_copy(step).wait_recv()

    for group in range(groups):
        lanes = slice(group * HEAD_DIM, (group + 1) * HEAD_DIM)
        piece = og_in[:, lanes]
        og_rows[group * BLOCK:(group + 1) * BLOCK, :] = piece
        piece_t = piece.T
        og_t[group] = piece_t
        inverse = 1.0 / sum_run[group]
        sum_run[group] = inverse
        attended = (out_acc[group] * inverse).astype(BF16)
        delta[group] = jnp.sum(piece_t.astype(F32) * attended.astype(F32), axis=0, keepdims=True)
        attn_send[:, lanes] = attended.T
        qgrad_acc[group] = jnp.zeros((HEAD_DIM, BLOCK), F32)

    def attn_copy(step):
        peer = lax.rem(h + step, head_count)
        return remote(
            attn_send.at[token_rows(peer), :], attn_recv.at[:, columns(h)],
            attn_send_sem.at[step], attn_recv_sem.at[step], (s, peer))

    def qgrad_copy(step, part):
        peer = lax.rem(h + step, head_count)
        return remote(
            qgrad_send.at[token_rows(peer), half_columns(0, part)], qgrad_recv.at[:, half_columns(h, part)],
            qgrad_send_sem.at[part, step], qgrad_recv_sem.at[part, step], (s, peer))

    def own_copy(source, target, sem):
        return pltpu.make_async_copy(source.at[token_rows(h), :], target.at[:, columns(h)], sem)

    for step in range(1, head_count):
        attn_copy(step).start()
    own_copy(attn_send, attn_recv, place_sem.at[0]).start()

    def grad_copy(j, kind):
        return remote(
            grad_send.at[j, kind], contrib.at[j, kind], grad_send_sem.at[j, kind], grad_recv_sem.at[j, kind],
            (s - (j - 1), h))

    def back_copy(kind):
        return remote(
            grad_send.at[2, kind], relay_grad.at[kind], back_send_sem.at[kind], back_recv_sem.at[kind],
            (s - RING, h))

    def pass_back(kind):
        return remote(
            relay_grad.at[kind], contrib.at[2, kind], pass_back_sem.at[kind], grad_recv_sem.at[2, kind],
            (s + (RING - 1), h))

    def grad_local(j):
        return pltpu.make_async_copy(grad_send.at[j], contrib.at[j], place_sem.at[2 + j])

    def backward_tile(j, group):
        factor = jnp.exp2((max_hist[j, group] - max_run[group]) * EXP2_SCALE) * sum_run[group]
        weights = expo[j, group] * factor
        weight_grad = matmul(value_slots[j], og_t[group])
        score_grad = (weights * (weight_grad - delta[group])).astype(BF16)
        qgrad_acc[group] += matmul(key_t[j], score_grad)
        return weights.astype(BF16), score_grad

    def query_lanes(group):
        return slice(group * BLOCK, (group + 1) * BLOCK)

    def backward_slot(j, carry):
        @pl.when(s >= j - 1)
        def _():
            for group in range(groups):
                weights, score_grad = backward_tile(j, group)
                weights_low[0, :, query_lanes(group)] = weights
                scores_low[0, :, query_lanes(group)] = score_grad
            grad_send[j, 0] = (matmul(scores_low[0], q_rows[...]) * SCALE).astype(BF16)
            grad_send[j, 1] = matmul(weights_low[0], og_rows[...]).astype(BF16)
            for kind in range(2):
                @pl.when(back_out & (j == 2))
                def _():
                    back_copy(kind).start()

                @pl.when(jnp.logical_not(back_out & (j == 2)))
                def _():
                    grad_copy(j, kind).start()
        return carry

    lax.fori_loop(2, SLOTS, backward_slot, 0)

    def local_back(part, carry):
        @pl.when(back_in)
        def _():
            for kind in range(2):
                @pl.when(part == kind)
                def _():
                    back_copy(kind).wait_recv()
                    pass_back(kind).start()
        for j in range(2):
            for member in range(pair):
                group = part * pair + member
                weights, score_grad = backward_tile(j, group)
                lanes = pl.ds(pl.multiple_of(group * BLOCK, BLOCK), BLOCK)
                weights_low[j, :, lanes] = weights
                scores_low[j, :, lanes] = score_grad
        for member in range(pair):
            group = part * pair + member
            qgrad_send[:, pl.ds(pl.multiple_of(group * HEAD_DIM, HEAD_DIM), HEAD_DIM)] = (
                qgrad_acc[group] * SCALE).astype(BF16).T
        for step in range(1, head_count):
            qgrad_copy(step, part).start()
        return carry

    lax.fori_loop(0, HALVES, local_back, 0)
    own_copy(qgrad_send, qgrad_recv, place_sem.at[1]).start()
    for j in range(2):
        grad_send[j, 0] = (matmul(scores_low[j], q_rows[...]) * SCALE).astype(BF16)
        grad_send[j, 1] = matmul(weights_low[j], og_rows[...]).astype(BF16)
        grad_local(j).start()

    for step in range(1, head_count):
        og_copy(step).wait_send()
        attn_copy(step).wait()
        for part in range(HALVES):
            q_copy(step, part).wait_send()
    for distance in range(1, PICKS):
        @pl.when(s >= distance)
        def _():
            sel_copy(distance).wait_send()
    for kind in range(2):
        @pl.when(relay_out)
        def _():
            relay_copy(kind).wait_send()

        @pl.when(jnp.logical_not(relay_out) & (s + 1 < seq_count))
        def _():
            kv_copy(1, kind).wait_send()

        @pl.when(relay_in)
        def _():
            pass_copy(kind).wait_send()

        @pl.when(back_out)
        def _():
            back_copy(kind).wait_send()

        @pl.when(jnp.logical_not(back_out) & (s >= 1))
        def _():
            grad_copy(2, kind).wait_send()

        @pl.when(back_in)
        def _():
            pass_back(kind).wait_send()

        for distance in range(2, PICKS):
            @pl.when(s + distance < seq_count)
            def _():
                kv_copy(distance, kind).wait_send()

            @pl.when(s >= distance)
            def _():
                grad_copy(distance + 1, kind).wait_send()
        for distance in range(1, PICKS):
            @pl.when(s + distance < seq_count)
            def _():
                grad_copy(distance + 1, kind).wait_recv()
    grad_local(0).wait()
    grad_local(1).wait()
    own_copy(attn_send, attn_recv, place_sem.at[0]).wait()
    own_copy(qgrad_send, qgrad_recv, place_sem.at[1]).wait()
    for part in range(HALVES):
        for step in range(1, head_count):
            qgrad_copy(step, part).wait()


def place_kernel(
    shard_blocks, target_ref, contrib, attn_in, qgrad_in,
    attn_out, qgrad_out, key_out, value_out,
    zeros, pieces, attn_buf, qgrad_buf, zero_sem, in_sem, out_sem, piece_in_sem, piece_out_sem,
):
    outs = (key_out, value_out)
    attn_load = pltpu.make_async_copy(attn_in, attn_buf, in_sem.at[0])
    qgrad_load = pltpu.make_async_copy(qgrad_in, qgrad_buf, in_sem.at[1])
    attn_load.start()
    qgrad_load.start()

    def piece_load(slot):
        return pltpu.make_async_copy(contrib.at[slot], pieces.at[slot], piece_in_sem.at[slot])

    targets = [target_ref[slot] for slot in range(SLOTS)]
    valid = [target >= 0 for target in targets]
    for slot in range(SLOTS):
        @pl.when(valid[slot])
        def _():
            piece_load(slot).start()

    zeros[...] = jnp.zeros_like(zeros)

    def taken(block):
        hit = targets[0] == block
        for slot in range(1, SLOTS):
            hit = hit | (targets[slot] == block)
        return hit

    def rows_of(block):
        return pl.ds(pl.multiple_of(block * BLOCK, BLOCK), BLOCK)

    def zero_copy(block, kind):
        return pltpu.make_async_copy(zeros, outs[kind].at[rows_of(block), :], zero_sem.at[kind, block])

    def zero_start(block, carry):
        @pl.when(jnp.logical_not(taken(block)))
        def _():
            zero_copy(block, 0).start()
            zero_copy(block, 1).start()
        return carry

    lax.fori_loop(0, shard_blocks, zero_start, 0)

    attn_store = pltpu.make_async_copy(attn_buf, attn_out, out_sem.at[0])
    qgrad_store = pltpu.make_async_copy(qgrad_buf, qgrad_out, out_sem.at[1])
    attn_load.wait()
    attn_store.start()
    qgrad_load.wait()
    qgrad_store.start()

    for slot in range(SLOTS):
        @pl.when(valid[slot])
        def _():
            piece_load(slot).wait()

    leads = []
    for slot in range(SLOTS):
        lead = valid[slot]
        for earlier in range(slot):
            lead = lead & jnp.logical_not(targets[earlier] == targets[slot])
        leads.append(lead)

    def piece_store(slot, kind):
        return pltpu.make_async_copy(
            pieces.at[slot, kind], outs[kind].at[rows_of(targets[slot]), :], piece_out_sem.at[slot, kind])

    for slot in range(SLOTS):
        @pl.when(leads[slot])
        def _():
            repeats = jnp.int32(0)
            for later in range(slot + 1, SLOTS):
                repeats = repeats + jnp.where(targets[later] == targets[slot], 1, 0)

            @pl.when(repeats > 0)
            def _():
                total = pieces[slot].astype(F32)
                for later in range(slot + 1, SLOTS):
                    total = total + jnp.where(targets[later] == targets[slot], pieces[later].astype(F32), 0.0)
                pieces[slot] = total.astype(BF16)
            piece_store(slot, 0).start()
            piece_store(slot, 1).start()

    def zero_wait(block, carry):
        @pl.when(jnp.logical_not(taken(block)))
        def _():
            zero_copy(block, 0).wait()
            zero_copy(block, 1).wait()
        return carry

    lax.fori_loop(0, shard_blocks, zero_wait, 0)
    for slot in range(SLOTS):
        @pl.when(leads[slot])
        def _():
            piece_store(slot, 0).wait()
            piece_store(slot, 1).wait()
    attn_store.wait()
    qgrad_store.wait()


def per_device(query, keys, values, out_grad, span_pos, selected):
    seq_count = lax.axis_size("seq")
    head_count = lax.axis_size("head")
    shard_blocks = keys.shape[0] // BLOCK
    rows, features = query.shape
    width = features // head_count
    groups = width // HEAD_DIM
    any_spec = pl.BlockSpec(memory_space=pl.ANY)
    smem_spec = pl.BlockSpec(memory_space=pltpu.SMEM)
    dma = pltpu.SemaphoreType.DMA
    contrib, attn_recv, qgrad_recv, targets = pl.pallas_call(
        functools.partial(attend_kernel, seq_count, head_count, groups, shard_blocks),
        out_shape=(
            jax.ShapeDtypeStruct((SLOTS, 2, BLOCK, HEAD_DIM), BF16),
            jax.ShapeDtypeStruct(query.shape, BF16),
            jax.ShapeDtypeStruct(query.shape, BF16),
            jax.ShapeDtypeStruct((8,), jnp.int32),
        ),
        in_specs=[smem_spec, smem_spec] + [any_spec] * 4,
        out_specs=(any_spec, any_spec, any_spec, smem_spec),
        scratch_shapes=[
            pltpu.SMEM((PICKS - 1, 1, PICKS), jnp.int32),
            pltpu.VMEM((shard_blocks, BLOCK, HEAD_DIM), BF16),
            pltpu.VMEM((shard_blocks, BLOCK, HEAD_DIM), BF16),
            pltpu.VMEM((BLOCK, width), BF16),
            pltpu.VMEM((BLOCK, width), BF16),
            pltpu.VMEM((groups * BLOCK, HEAD_DIM), BF16),
            pltpu.VMEM((groups * BLOCK, HEAD_DIM), BF16),
            pltpu.VMEM((groups, HEAD_DIM, BLOCK), BF16),
            pltpu.VMEM((groups, HEAD_DIM, BLOCK), BF16),
            pltpu.VMEM((SLOTS, BLOCK, HEAD_DIM), BF16),
            pltpu.VMEM((SLOTS, BLOCK, HEAD_DIM), BF16),
            pltpu.VMEM((SLOTS, HEAD_DIM, BLOCK), BF16),
            pltpu.VMEM((SLOTS, HEAD_DIM, BLOCK), BF16),
            pltpu.VMEM((PICKS - 1, 2, BLOCK, HEAD_DIM), BF16),
            pltpu.VMEM((SLOTS, 2, BLOCK, HEAD_DIM), BF16),
            pltpu.VMEM((2, BLOCK, HEAD_DIM), BF16),
            pltpu.VMEM((2, BLOCK, HEAD_DIM), BF16),
            pltpu.VMEM((SLOTS, groups, BLOCK, BLOCK), F32),
            pltpu.VMEM((SLOTS, groups, 1, BLOCK), F32),
            pltpu.VMEM((groups, 1, BLOCK), F32),
            pltpu.VMEM((groups, 1, BLOCK), F32),
            pltpu.VMEM((groups, 1, BLOCK), F32),
            pltpu.VMEM((groups, HEAD_DIM, BLOCK), F32),
            pltpu.VMEM((groups, HEAD_DIM, BLOCK), F32),
            pltpu.VMEM((2, BLOCK, groups * BLOCK), BF16),
            pltpu.VMEM((2, BLOCK, groups * BLOCK), BF16),
            pltpu.VMEM((BLOCK, width), BF16),
            pltpu.VMEM((BLOCK, width), BF16),
            dma((4,)),
            dma((PICKS - 1,)), dma((PICKS - 1,)),
            dma((HALVES, head_count)), dma((HALVES, head_count)),
            dma((head_count,)), dma((head_count,)),
            dma((PICKS - 1, 2)), dma((PICKS - 1, 2)),
            dma((2,)), dma((2,)), dma((2,)),
            dma((SLOTS, 2)), dma((SLOTS, 2)),
            dma((2,)), dma((2,)), dma((2,)),
            dma((head_count,)), dma((head_count,)),
            dma((HALVES, head_count)), dma((HALVES, head_count)),
            dma((4,)),
        ],
        compiler_params=pltpu.CompilerParams(
            collective_id=0, has_side_effects=True, vmem_limit_bytes=56 * 1024 * 1024),
        name="attend",
    )(selected, span_pos, query, out_grad,
      keys.reshape(shard_blocks, BLOCK, HEAD_DIM), values.reshape(shard_blocks, BLOCK, HEAD_DIM))

    return pl.pallas_call(
        functools.partial(place_kernel, shard_blocks),
        out_shape=(
            jax.ShapeDtypeStruct(query.shape, BF16),
            jax.ShapeDtypeStruct(query.shape, BF16),
            jax.ShapeDtypeStruct(keys.shape, BF16),
            jax.ShapeDtypeStruct(values.shape, BF16),
        ),
        in_specs=[smem_spec, any_spec, any_spec, any_spec],
        out_specs=(any_spec,) * 4,
        scratch_shapes=[
            pltpu.VMEM((BLOCK, HEAD_DIM), BF16),
            pltpu.VMEM((SLOTS, 2, BLOCK, HEAD_DIM), BF16),
            pltpu.VMEM(query.shape, BF16),
            pltpu.VMEM(query.shape, BF16),
            dma((2, shard_blocks)),
            dma((2,)),
            dma((2,)),
            dma((SLOTS,)),
            dma((SLOTS, 2)),
        ],
        name="place",
    )(targets, contrib, attn_recv, qgrad_recv)


def solution(mesh):
    in_specs = (
        P(("seq", "head"), None),
        P("seq", "head"),
        P("seq", "head"),
        P(("seq", "head"), None),
        P("seq"),
        P("seq", None),
    )
    out_specs = (
        P(("seq", "head"), None),
        P(("seq", "head"), None),
        P("seq", "head"),
        P("seq", "head"),
    )
    return jax.shard_map(
        per_device, mesh=mesh, in_specs=in_specs, out_specs=out_specs, check_vma=False
    )
```

```python
import functools

import jax
import jax.numpy as jnp
from jax import lax
from jax.experimental import pallas as pl
from jax.experimental.pallas import tpu as pltpu
from jax.sharding import PartitionSpec as P

HEAD_DIM = 128
BLOCK = 512
PICKS = 4
SLOTS = PICKS + 1
RING = 4
HALVES = 2
SCALE = HEAD_DIM ** -0.5
EXP2_SCALE = SCALE * 1.4426950408889634
MASKED = -1e30
MESH = pl.DeviceIdType.MESH
F32 = jnp.float32
BF16 = jnp.bfloat16


def matmul(left, right):
    return jnp.dot(left, right, preferred_element_type=F32)


def attend_kernel(
    seq_count, head_count, groups, shard_blocks,
    sel_ref, pos_ref, q_hbm, og_hbm, k_hbm, v_hbm,
    contrib, attn_recv, qgrad_recv, target_ref,
    sel_recv, k_all, v_all, q_in, og_in, q_rows, og_rows, q_t, og_t,
    key_slots, value_slots, key_t, value_t, kv_send, grad_send, relay_kv, relay_grad, expo,
    max_hist, max_run, sum_run, delta, out_acc, qgrad_acc, weights_low, scores_low, attn_send, qgrad_send,
    load_sem, sel_send_sem, sel_recv_sem, q_send_sem, q_recv_sem, og_send_sem, og_recv_sem,
    kv_send_sem, kv_recv_sem, relay_send_sem, relay_recv_sem, pass_send_sem,
    grad_send_sem, grad_recv_sem, back_send_sem, back_recv_sem, pass_back_sem,
    attn_send_sem, attn_recv_sem, qgrad_send_sem, qgrad_recv_sem, place_sem,
):
    s = lax.axis_index("seq")
    h = lax.axis_index("head")
    width = groups * HEAD_DIM
    half = width // HALVES
    pair = groups // HALVES
    rows = q_hbm.shape[0]
    column = lax.rem(s, RING)
    relay_out = (column == RING - 1) & (s + 1 < seq_count)
    relay_in = (column == RING - 1) & (s >= RING)
    back_out = s < 0
    back_in = s < 0

    def columns(index):
        return pl.ds(pl.multiple_of(index * width, width), width)

    def half_columns(index, part):
        return pl.ds(pl.multiple_of(index * width + part * half, half), half)

    def token_rows(index):
        return pl.ds(pl.multiple_of(index * rows, rows), rows)

    load_k = pltpu.make_async_copy(k_hbm, k_all, load_sem.at[0])
    load_v = pltpu.make_async_copy(v_hbm, v_all, load_sem.at[1])
    load_q = pltpu.make_async_copy(q_hbm.at[:, columns(h)], q_in.at[token_rows(h), :], load_sem.at[2])
    load_og = pltpu.make_async_copy(og_hbm.at[:, columns(h)], og_in.at[token_rows(h), :], load_sem.at[3])
    load_q.start()
    load_k.start()
    load_v.start()
    load_og.start()

    barrier = pltpu.get_barrier_semaphore()
    for step in range(1, head_count):
        peer = lax.rem(h + step, head_count)
        pl.semaphore_signal(barrier, inc=1, device_id=(s, peer), device_id_type=MESH)
    for distance in range(1, RING + 1):
        for other in (lax.rem(s + distance, seq_count), lax.rem(s + seq_count - distance, seq_count)):
            pl.semaphore_signal(barrier, inc=1, device_id=(other, h), device_id_type=MESH)
    pl.semaphore_wait(barrier, head_count - 1 + 2 * RING)

    def remote(source, target, send_sem, recv_sem, device):
        return pltpu.make_async_remote_copy(
            src_ref=source, dst_ref=target, send_sem=send_sem, recv_sem=recv_sem,
            device_id=device, device_id_type=MESH)

    def sel_copy(distance):
        return remote(
            sel_ref, sel_recv.at[distance - 1], sel_send_sem.at[distance - 1],
            sel_recv_sem.at[distance - 1], (s - distance, h))

    for distance in range(1, PICKS):
        @pl.when(s >= distance)
        def _():
            sel_copy(distance).start()

    def q_copy(step, part):
        peer = lax.rem(h + step, head_count)
        return remote(
            q_hbm.at[:, half_columns(peer, part)], q_in.at[token_rows(h), half_columns(0, part)],
            q_send_sem.at[part, step], q_recv_sem.at[part, step], (s, peer))

    def og_copy(step):
        peer = lax.rem(h + step, head_count)
        return remote(
            og_hbm.at[:, columns(peer)], og_in.at[token_rows(h), :],
            og_send_sem.at[step], og_recv_sem.at[step], (s, peer))

    for part in range(HALVES):
        for step in range(1, head_count):
            q_copy(step, part).start()
    for step in range(1, head_count):
        og_copy(step).start()

    load_k.wait()
    load_v.wait()
    slots = (key_slots, value_slots)

    def kv_copy(distance, kind):
        return remote(
            kv_send.at[distance - 1, kind], slots[kind].at[distance + 1],
            kv_send_sem.at[distance - 1, kind], kv_recv_sem.at[distance - 1, kind], (s + distance, h))

    def relay_copy(kind):
        return remote(
            kv_send.at[0, kind], relay_kv.at[kind], relay_send_sem.at[kind], relay_recv_sem.at[kind],
            (s + RING, h))

    def pass_copy(kind):
        return remote(
            relay_kv.at[kind], slots[kind].at[2], pass_send_sem.at[kind], kv_recv_sem.at[0, kind],
            (s - (RING - 1), h))

    for distance in range(1, PICKS):
        target_ref[distance + 1] = jnp.int32(-1)

        @pl.when(s + distance < seq_count)
        def _():
            sel_copy(distance).wait_recv()
            entry = lax.rem(sel_recv[distance - 1, 0, distance], shard_blocks)
            target_ref[distance + 1] = entry
            for kind in (1, 0):
                kv_send[distance - 1, kind] = (k_all, v_all)[kind][entry]
                if distance == 1 and kind == 1:
                    @pl.when(relay_out)
                    def _():
                        relay_copy(kind).start()

                    @pl.when(jnp.logical_not(relay_out))
                    def _():
                        kv_copy(1, kind).start()
                else:
                    kv_copy(distance, kind).start()

    own_entry = lax.rem(pos_ref[0], shard_blocks)
    first_entry = lax.rem(sel_ref[0, 0], shard_blocks)
    target_ref[0] = own_entry
    target_ref[1] = first_entry

    def transpose_slot(j):
        key_t[j] = key_slots[j].T
        value_t[j] = value_slots[j].T

    for j, entry in enumerate((own_entry, first_entry)):
        key_slots[j] = k_all[entry]
        value_slots[j] = v_all[entry]
        transpose_slot(j)

    def forward_first(group):
        scores = matmul(key_slots[0], q_t[group])
        key_pos = lax.broadcasted_iota(jnp.int32, scores.shape, 0)
        query_pos = lax.broadcasted_iota(jnp.int32, scores.shape, 1)
        scores = jnp.where(key_pos <= query_pos, scores, MASKED)
        new_max = jnp.max(scores, axis=0, keepdims=True)
        exponent = jnp.exp2((scores - new_max) * EXP2_SCALE)
        expo[0, group] = exponent
        max_hist[0, group] = new_max
        max_run[group] = new_max
        sum_run[group] = jnp.sum(exponent, axis=0, keepdims=True)
        out_acc[group] = matmul(value_t[0], exponent.astype(BF16))

    def forward_next(j, group):
        scores = matmul(key_slots[j], q_t[group])
        old_max = max_run[group]
        new_max = jnp.maximum(old_max, jnp.max(scores, axis=0, keepdims=True))
        exponent = jnp.exp2((scores - new_max) * EXP2_SCALE)
        expo[j, group] = exponent
        max_hist[j, group] = new_max
        max_run[group] = new_max
        fade = jnp.exp2((old_max - new_max) * EXP2_SCALE)
        sum_run[group] = sum_run[group] * fade + jnp.sum(exponent, axis=0, keepdims=True)
        out_acc[group] = out_acc[group] * fade + matmul(value_t[j], exponent.astype(BF16))

    @pl.when(relay_in)
    def _():
        relay_copy(1).wait_recv()
        pass_copy(1).start()

    load_q.wait()

    def local_part(part, carry):
        for step in range(1, head_count):
            q_copy(step, part).wait_recv()
        for member in range(pair):
            group = part * pair + member
            piece = q_in[:, pl.ds(pl.multiple_of(group * HEAD_DIM, HEAD_DIM), HEAD_DIM)]
            q_rows[pl.ds(pl.multiple_of(group * BLOCK, BLOCK), BLOCK), :] = piece
            q_t[group] = piece.T
        for member in range(pair):
            forward_first(part * pair + member)
        for member in range(pair):
            forward_next(1, part * pair + member)
        return carry

    lax.fori_loop(0, HALVES, local_part, 0)

    def forward_slot(j, carry):
        @pl.when(s >= j - 1)
        def _():
            for kind in range(2):
                remote(
                    kv_send.at[j - 2, kind], slots[kind].at[j], kv_send_sem.at[j - 2, kind],
                    kv_recv_sem.at[j - 2, kind], (s, h)).wait_recv()
            transpose_slot(j)
            for group in range(groups):
                forward_next(j, group)
        return carry

    lax.fori_loop(2, SLOTS, forward_slot, 0)

    load_og.wait()
    for step in range(1, head_count):
        og_copy(step).wait_recv()

    for group in range(groups):
        lanes = slice(group * HEAD_DIM, (group + 1) * HEAD_DIM)
        piece = og_in[:, lanes]
        og_rows[group * BLOCK:(group + 1) * BLOCK, :] = piece
        piece_t = piece.T
        og_t[group] = piece_t
        inverse = 1.0 / sum_run[group]
        sum_run[group] = inverse
        attended = (out_acc[group] * inverse).astype(BF16)
        delta[group] = jnp.sum(piece_t.astype(F32) * attended.astype(F32), axis=0, keepdims=True)
        attn_send[:, lanes] = attended.T
        qgrad_acc[group] = jnp.zeros((HEAD_DIM, BLOCK), F32)

    def attn_copy(step):
        peer = lax.rem(h + step, head_count)
        return remote(
            attn_send.at[token_rows(peer), :], attn_recv.at[:, columns(h)],
            attn_send_sem.at[step], attn_recv_sem.at[step], (s, peer))

    def qgrad_copy(step, part):
        peer = lax.rem(h + step, head_count)
        return remote(
            qgrad_send.at[token_rows(peer), half_columns(0, part)], qgrad_recv.at[:, half_columns(h, part)],
            qgrad_send_sem.at[part, step], qgrad_recv_sem.at[part, step], (s, peer))

    def own_copy(source, target, sem):
        return pltpu.make_async_copy(source.at[token_rows(h), :], target.at[:, columns(h)], sem)

    for step in range(1, head_count):
        attn_copy(step).start()
    own_copy(attn_send, attn_recv, place_sem.at[0]).start()

    def grad_copy(j, kind):
        return remote(
            grad_send.at[j, kind], contrib.at[j, kind], grad_send_sem.at[j, kind], grad_recv_sem.at[j, kind],
            (s - (j - 1), h))

    def back_copy(kind):
        return remote(
            grad_send.at[2, kind], relay_grad.at[kind], back_send_sem.at[kind], back_recv_sem.at[kind],
            (s - RING, h))

    def pass_back(kind):
        return remote(
            relay_grad.at[kind], contrib.at[2, kind], pass_back_sem.at[kind], grad_recv_sem.at[2, kind],
            (s + (RING - 1), h))

    def grad_local(j):
        return pltpu.make_async_copy(grad_send.at[j], contrib.at[j], place_sem.at[2 + j])

    def backward_tile(j, group):
        factor = jnp.exp2((max_hist[j, group] - max_run[group]) * EXP2_SCALE) * sum_run[group]
        weights = expo[j, group] * factor
        weight_grad = matmul(value_slots[j], og_t[group])
        score_grad = (weights * (weight_grad - delta[group])).astype(BF16)
        qgrad_acc[group] += matmul(key_t[j], score_grad)
        return weights.astype(BF16), score_grad

    def query_lanes(group):
        return slice(group * BLOCK, (group + 1) * BLOCK)

    def backward_slot(j, carry):
        @pl.when(s >= j - 1)
        def _():
            for group in range(groups):
                weights, score_grad = backward_tile(j, group)
                weights_low[0, :, query_lanes(group)] = weights
                scores_low[0, :, query_lanes(group)] = score_grad
            grad_send[j, 0] = (matmul(scores_low[0], q_rows[...]) * SCALE).astype(BF16)
            grad_send[j, 1] = matmul(weights_low[0], og_rows[...]).astype(BF16)
            for kind in range(2):
                @pl.when(back_out & (j == 2))
                def _():
                    back_copy(kind).start()

                @pl.when(jnp.logical_not(back_out & (j == 2)))
                def _():
                    grad_copy(j, kind).start()
        return carry

    lax.fori_loop(2, SLOTS, backward_slot, 0)

    def local_back(part, carry):
        @pl.when(back_in)
        def _():
            for kind in range(2):
                @pl.when(part == min(kind, HALVES - 1))
                def _():
                    back_copy(kind).wait_recv()
                    pass_back(kind).start()
        for j in range(2):
            for member in range(pair):
                group = part * pair + member
                weights, score_grad = backward_tile(j, group)
                lanes = pl.ds(pl.multiple_of(group * BLOCK, BLOCK), BLOCK)
                weights_low[j, :, lanes] = weights
                scores_low[j, :, lanes] = score_grad
        for member in range(pair):
            group = part * pair + member
            qgrad_send[:, pl.ds(pl.multiple_of(group * HEAD_DIM, HEAD_DIM), HEAD_DIM)] = (
                qgrad_acc[group] * SCALE).astype(BF16).T
        for step in range(1, head_count):
            qgrad_copy(step, part).start()
        return carry

    lax.fori_loop(0, HALVES, local_back, 0)
    own_copy(qgrad_send, qgrad_recv, place_sem.at[1]).start()
    for j in range(2):
        grad_send[j, 0] = (matmul(scores_low[j], q_rows[...]) * SCALE).astype(BF16)
        grad_send[j, 1] = matmul(weights_low[j], og_rows[...]).astype(BF16)
        grad_local(j).start()

    for step in range(1, head_count):
        og_copy(step).wait_send()
        attn_copy(step).wait()
        for part in range(HALVES):
            q_copy(step, part).wait_send()
    for distance in range(1, PICKS):
        @pl.when(s >= distance)
        def _():
            sel_copy(distance).wait_send()
    for kind in range(2):
        if kind == 1:
            @pl.when(relay_out)
            def _():
                relay_copy(kind).wait_send()

            @pl.when(relay_in)
            def _():
                pass_copy(kind).wait_send()

            @pl.when(jnp.logical_not(relay_out) & (s + 1 < seq_count))
            def _():
                kv_copy(1, kind).wait_send()
        else:
            @pl.when(s + 1 < seq_count)
            def _():
                kv_copy(1, kind).wait_send()

        @pl.when(back_out)
        def _():
            back_copy(kind).wait_send()

        @pl.when(jnp.logical_not(back_out) & (s >= 1))
        def _():
            grad_copy(2, kind).wait_send()

        @pl.when(back_in)
        def _():
            pass_back(kind).wait_send()

        for distance in range(2, PICKS):
            @pl.when(s + distance < seq_count)
            def _():
                kv_copy(distance, kind).wait_send()

            @pl.when(s >= distance)
            def _():
                grad_copy(distance + 1, kind).wait_send()
        for distance in range(1, PICKS):
            @pl.when(s + distance < seq_count)
            def _():
                grad_copy(distance + 1, kind).wait_recv()
    grad_local(0).wait()
    grad_local(1).wait()
    own_copy(attn_send, attn_recv, place_sem.at[0]).wait()
    own_copy(qgrad_send, qgrad_recv, place_sem.at[1]).wait()
    for part in range(HALVES):
        for step in range(1, head_count):
            qgrad_copy(step, part).wait()


def place_kernel(
    shard_blocks, target_ref, contrib, attn_in, qgrad_in,
    attn_out, qgrad_out, key_out, value_out,
    zeros, pieces, attn_buf, qgrad_buf, zero_sem, in_sem, out_sem, piece_in_sem, piece_out_sem,
):
    outs = (key_out, value_out)
    attn_load = pltpu.make_async_copy(attn_in, attn_buf, in_sem.at[0])
    qgrad_load = pltpu.make_async_copy(qgrad_in, qgrad_buf, in_sem.at[1])
    attn_load.start()
    qgrad_load.start()

    def piece_load(slot):
        return pltpu.make_async_copy(contrib.at[slot], pieces.at[slot], piece_in_sem.at[slot])

    targets = [target_ref[slot] for slot in range(SLOTS)]
    valid = [target >= 0 for target in targets]
    for slot in range(SLOTS):
        @pl.when(valid[slot])
        def _():
            piece_load(slot).start()

    zeros[...] = jnp.zeros_like(zeros)

    def taken(block):
        hit = targets[0] == block
        for slot in range(1, SLOTS):
            hit = hit | (targets[slot] == block)
        return hit

    def rows_of(block):
        return pl.ds(pl.multiple_of(block * BLOCK, BLOCK), BLOCK)

    def zero_copy(block, kind):
        return pltpu.make_async_copy(zeros, outs[kind].at[rows_of(block), :], zero_sem.at[kind, block])

    def zero_start(block, carry):
        @pl.when(jnp.logical_not(taken(block)))
        def _():
            zero_copy(block, 0).start()
            zero_copy(block, 1).start()
        return carry

    lax.fori_loop(0, shard_blocks, zero_start, 0)

    attn_store = pltpu.make_async_copy(attn_buf, attn_out, out_sem.at[0])
    qgrad_store = pltpu.make_async_copy(qgrad_buf, qgrad_out, out_sem.at[1])
    attn_load.wait()
    attn_store.start()
    qgrad_load.wait()
    qgrad_store.start()

    for slot in range(SLOTS):
        @pl.when(valid[slot])
        def _():
            piece_load(slot).wait()

    leads = []
    for slot in range(SLOTS):
        lead = valid[slot]
        for earlier in range(slot):
            lead = lead & jnp.logical_not(targets[earlier] == targets[slot])
        leads.append(lead)

    def piece_store(slot, kind):
        return pltpu.make_async_copy(
            pieces.at[slot, kind], outs[kind].at[rows_of(targets[slot]), :], piece_out_sem.at[slot, kind])

    for slot in range(SLOTS):
        @pl.when(leads[slot])
        def _():
            repeats = jnp.int32(0)
            for later in range(slot + 1, SLOTS):
                repeats = repeats + jnp.where(targets[later] == targets[slot], 1, 0)

            @pl.when(repeats > 0)
            def _():
                total = pieces[slot].astype(F32)
                for later in range(slot + 1, SLOTS):
                    total = total + jnp.where(targets[later] == targets[slot], pieces[later].astype(F32), 0.0)
                pieces[slot] = total.astype(BF16)
            piece_store(slot, 0).start()
            piece_store(slot, 1).start()

    def zero_wait(block, carry):
        @pl.when(jnp.logical_not(taken(block)))
        def _():
            zero_copy(block, 0).wait()
            zero_copy(block, 1).wait()
        return carry

    lax.fori_loop(0, shard_blocks, zero_wait, 0)
    for slot in range(SLOTS):
        @pl.when(leads[slot])
        def _():
            piece_store(slot, 0).wait()
            piece_store(slot, 1).wait()
    attn_store.wait()
    qgrad_store.wait()


def per_device(query, keys, values, out_grad, span_pos, selected):
    seq_count = lax.axis_size("seq")
    head_count = lax.axis_size("head")
    shard_blocks = keys.shape[0] // BLOCK
    rows, features = query.shape
    width = features // head_count
    groups = width // HEAD_DIM
    any_spec = pl.BlockSpec(memory_space=pl.ANY)
    smem_spec = pl.BlockSpec(memory_space=pltpu.SMEM)
    dma = pltpu.SemaphoreType.DMA
    contrib, attn_recv, qgrad_recv, targets = pl.pallas_call(
        functools.partial(attend_kernel, seq_count, head_count, groups, shard_blocks),
        out_shape=(
            jax.ShapeDtypeStruct((SLOTS, 2, BLOCK, HEAD_DIM), BF16),
            jax.ShapeDtypeStruct(query.shape, BF16),
            jax.ShapeDtypeStruct(query.shape, BF16),
            jax.ShapeDtypeStruct((8,), jnp.int32),
        ),
        in_specs=[smem_spec, smem_spec] + [any_spec] * 4,
        out_specs=(any_spec, any_spec, any_spec, smem_spec),
        scratch_shapes=[
            pltpu.SMEM((PICKS - 1, 1, PICKS), jnp.int32),
            pltpu.VMEM((shard_blocks, BLOCK, HEAD_DIM), BF16),
            pltpu.VMEM((shard_blocks, BLOCK, HEAD_DIM), BF16),
            pltpu.VMEM((BLOCK, width), BF16),
            pltpu.VMEM((BLOCK, width), BF16),
            pltpu.VMEM((groups * BLOCK, HEAD_DIM), BF16),
            pltpu.VMEM((groups * BLOCK, HEAD_DIM), BF16),
            pltpu.VMEM((groups, HEAD_DIM, BLOCK), BF16),
            pltpu.VMEM((groups, HEAD_DIM, BLOCK), BF16),
            pltpu.VMEM((SLOTS, BLOCK, HEAD_DIM), BF16),
            pltpu.VMEM((SLOTS, BLOCK, HEAD_DIM), BF16),
            pltpu.VMEM((SLOTS, HEAD_DIM, BLOCK), BF16),
            pltpu.VMEM((SLOTS, HEAD_DIM, BLOCK), BF16),
            pltpu.VMEM((PICKS - 1, 2, BLOCK, HEAD_DIM), BF16),
            pltpu.VMEM((SLOTS, 2, BLOCK, HEAD_DIM), BF16),
            pltpu.VMEM((2, BLOCK, HEAD_DIM), BF16),
            pltpu.VMEM((2, BLOCK, HEAD_DIM), BF16),
            pltpu.VMEM((SLOTS, groups, BLOCK, BLOCK), F32),
            pltpu.VMEM((SLOTS, groups, 1, BLOCK), F32),
            pltpu.VMEM((groups, 1, BLOCK), F32),
            pltpu.VMEM((groups, 1, BLOCK), F32),
            pltpu.VMEM((groups, 1, BLOCK), F32),
            pltpu.VMEM((groups, HEAD_DIM, BLOCK), F32),
            pltpu.VMEM((groups, HEAD_DIM, BLOCK), F32),
            pltpu.VMEM((2, BLOCK, groups * BLOCK), BF16),
            pltpu.VMEM((2, BLOCK, groups * BLOCK), BF16),
            pltpu.VMEM((BLOCK, width), BF16),
            pltpu.VMEM((BLOCK, width), BF16),
            dma((4,)),
            dma((PICKS - 1,)), dma((PICKS - 1,)),
            dma((HALVES, head_count)), dma((HALVES, head_count)),
            dma((head_count,)), dma((head_count,)),
            dma((PICKS - 1, 2)), dma((PICKS - 1, 2)),
            dma((2,)), dma((2,)), dma((2,)),
            dma((SLOTS, 2)), dma((SLOTS, 2)),
            dma((2,)), dma((2,)), dma((2,)),
            dma((head_count,)), dma((head_count,)),
            dma((HALVES, head_count)), dma((HALVES, head_count)),
            dma((4,)),
        ],
        compiler_params=pltpu.CompilerParams(
            collective_id=0, has_side_effects=True, vmem_limit_bytes=56 * 1024 * 1024),
        name="attend",
    )(selected, span_pos, query, out_grad,
      keys.reshape(shard_blocks, BLOCK, HEAD_DIM), values.reshape(shard_blocks, BLOCK, HEAD_DIM))

    return pl.pallas_call(
        functools.partial(place_kernel, shard_blocks),
        out_shape=(
            jax.ShapeDtypeStruct(query.shape, BF16),
            jax.ShapeDtypeStruct(query.shape, BF16),
            jax.ShapeDtypeStruct(keys.shape, BF16),
            jax.ShapeDtypeStruct(values.shape, BF16),
        ),
        in_specs=[smem_spec, any_spec, any_spec, any_spec],
        out_specs=(any_spec,) * 4,
        scratch_shapes=[
            pltpu.VMEM((BLOCK, HEAD_DIM), BF16),
            pltpu.VMEM((SLOTS, 2, BLOCK, HEAD_DIM), BF16),
            pltpu.VMEM(query.shape, BF16),
            pltpu.VMEM(query.shape, BF16),
            dma((2, shard_blocks)),
            dma((2,)),
            dma((2,)),
            dma((SLOTS,)),
            dma((SLOTS, 2)),
        ],
        name="place",
    )(targets, contrib, attn_recv, qgrad_recv)


def solution(mesh):
    in_specs = (
        P(("seq", "head"), None),
        P("seq", "head"),
        P("seq", "head"),
        P(("seq", "head"), None),
        P("seq"),
        P("seq", None),
    )
    out_specs = (
        P(("seq", "head"), None),
        P(("seq", "head"), None),
        P("seq", "head"),
        P("seq", "head"),
    )
    return jax.shard_map(
        per_device, mesh=mesh, in_specs=in_specs, out_specs=out_specs, check_vma=False
    )
```

```python
import functools

import jax
import jax.numpy as jnp
from jax import lax
from jax.experimental import pallas as pl
from jax.experimental.pallas import tpu as pltpu
from jax.sharding import PartitionSpec as P

HEAD_DIM = 128
BLOCK = 512
PICKS = 4
SLOTS = PICKS + 1
RING = 4
HALVES = 2
CORNER = BLOCK // 2
SCALE = HEAD_DIM ** -0.5
EXP2_SCALE = SCALE * 1.4426950408889634
MASKED = -1e30
MESH = pl.DeviceIdType.MESH
F32 = jnp.float32
BF16 = jnp.bfloat16


def matmul(left, right):
    return jnp.dot(left, right, preferred_element_type=F32)


def attend_kernel(
    seq_count, head_count, groups, shard_blocks,
    sel_ref, pos_ref, q_hbm, og_hbm, k_hbm, v_hbm,
    contrib, attn_recv, qgrad_recv, target_ref,
    sel_recv, k_all, v_all, q_in, og_in, q_rows, og_rows, q_t, og_t,
    key_slots, value_slots, key_t, value_t, kv_send, grad_send, relay_kv, relay_grad, expo,
    max_hist, max_run, sum_run, delta, out_acc, qgrad_acc, weights_low, scores_low, attn_send, qgrad_send,
    load_sem, sel_send_sem, sel_recv_sem, q_send_sem, q_recv_sem, og_send_sem, og_recv_sem,
    kv_send_sem, kv_recv_sem, relay_send_sem, relay_recv_sem, pass_send_sem,
    grad_send_sem, grad_recv_sem, back_send_sem, back_recv_sem, pass_back_sem,
    attn_send_sem, attn_recv_sem, qgrad_send_sem, qgrad_recv_sem, place_sem,
):
    s = lax.axis_index("seq")
    h = lax.axis_index("head")
    width = groups * HEAD_DIM
    half = width // HALVES
    pair = groups // HALVES
    rows = q_hbm.shape[0]
    column = lax.rem(s, RING)
    relay_out = (column == RING - 1) & (s + 1 < seq_count)
    relay_in = (column == RING - 1) & (s >= RING)
    back_out = s < 0
    back_in = s < 0

    def columns(index):
        return pl.ds(pl.multiple_of(index * width, width), width)

    def half_columns(index, part):
        return pl.ds(pl.multiple_of(index * width + part * half, half), half)

    def token_rows(index):
        return pl.ds(pl.multiple_of(index * rows, rows), rows)

    load_k = pltpu.make_async_copy(k_hbm, k_all, load_sem.at[0])
    load_v = pltpu.make_async_copy(v_hbm, v_all, load_sem.at[1])
    load_q = pltpu.make_async_copy(q_hbm.at[:, columns(h)], q_in.at[token_rows(h), :], load_sem.at[2])
    load_og = pltpu.make_async_copy(og_hbm.at[:, columns(h)], og_in.at[token_rows(h), :], load_sem.at[3])
    load_q.start()
    load_k.start()
    load_v.start()
    load_og.start()

    barrier = pltpu.get_barrier_semaphore()
    for step in range(1, head_count):
        peer = lax.rem(h + step, head_count)
        pl.semaphore_signal(barrier, inc=1, device_id=(s, peer), device_id_type=MESH)
    for distance in range(1, RING + 1):
        for other in (lax.rem(s + distance, seq_count), lax.rem(s + seq_count - distance, seq_count)):
            pl.semaphore_signal(barrier, inc=1, device_id=(other, h), device_id_type=MESH)
    pl.semaphore_wait(barrier, head_count - 1 + 2 * RING)

    def remote(source, target, send_sem, recv_sem, device):
        return pltpu.make_async_remote_copy(
            src_ref=source, dst_ref=target, send_sem=send_sem, recv_sem=recv_sem,
            device_id=device, device_id_type=MESH)

    def sel_copy(distance):
        return remote(
            sel_ref, sel_recv.at[distance - 1], sel_send_sem.at[distance - 1],
            sel_recv_sem.at[distance - 1], (s - distance, h))

    for distance in range(1, PICKS):
        @pl.when(s >= distance)
        def _():
            sel_copy(distance).start()

    def q_copy(step, part):
        peer = lax.rem(h + step, head_count)
        return remote(
            q_hbm.at[:, half_columns(peer, part)], q_in.at[token_rows(h), half_columns(0, part)],
            q_send_sem.at[part, step], q_recv_sem.at[part, step], (s, peer))

    def og_copy(step):
        peer = lax.rem(h + step, head_count)
        return remote(
            og_hbm.at[:, columns(peer)], og_in.at[token_rows(h), :],
            og_send_sem.at[step], og_recv_sem.at[step], (s, peer))

    for part in range(HALVES):
        for step in range(1, head_count):
            q_copy(step, part).start()
    for step in range(1, head_count):
        og_copy(step).start()

    load_k.wait()
    load_v.wait()
    slots = (key_slots, value_slots)

    def kv_copy(distance, kind):
        return remote(
            kv_send.at[distance - 1, kind], slots[kind].at[distance + 1],
            kv_send_sem.at[distance - 1, kind], kv_recv_sem.at[distance - 1, kind], (s + distance, h))

    def relay_copy(kind):
        return remote(
            kv_send.at[0, kind], relay_kv.at[kind], relay_send_sem.at[kind], relay_recv_sem.at[kind],
            (s + RING, h))

    def pass_copy(kind):
        return remote(
            relay_kv.at[kind], slots[kind].at[2], pass_send_sem.at[kind], kv_recv_sem.at[0, kind],
            (s - (RING - 1), h))

    for distance in range(1, PICKS):
        target_ref[distance + 1] = jnp.int32(-1)

        @pl.when(s + distance < seq_count)
        def _():
            sel_copy(distance).wait_recv()
            entry = lax.rem(sel_recv[distance - 1, 0, distance], shard_blocks)
            target_ref[distance + 1] = entry
            for kind in (1, 0):
                kv_send[distance - 1, kind] = (k_all, v_all)[kind][entry]
                if distance == 1 and kind == 1:
                    @pl.when(relay_out)
                    def _():
                        relay_copy(kind).start()

                    @pl.when(jnp.logical_not(relay_out))
                    def _():
                        kv_copy(1, kind).start()
                else:
                    kv_copy(distance, kind).start()

    own_entry = lax.rem(pos_ref[0], shard_blocks)
    first_entry = lax.rem(sel_ref[0, 0], shard_blocks)
    target_ref[0] = own_entry
    target_ref[1] = first_entry

    def transpose_slot(j):
        key_t[j] = key_slots[j].T
        value_t[j] = value_slots[j].T

    for j, entry in enumerate((own_entry, first_entry)):
        key_slots[j] = k_all[entry]
        value_slots[j] = v_all[entry]
        transpose_slot(j)

    def forward_first(group):
        for top in (CORNER, BLOCK):
            lanes = slice(top - CORNER, top)
            scores = matmul(key_slots[0, :top, :], q_t[group, :, lanes])
            key_pos = lax.broadcasted_iota(jnp.int32, scores.shape, 0)
            query_pos = lax.broadcasted_iota(jnp.int32, scores.shape, 1) + (top - CORNER)
            scores = jnp.where(key_pos <= query_pos, scores, MASKED)
            new_max = jnp.max(scores, axis=0, keepdims=True)
            exponent = jnp.exp2((scores - new_max) * EXP2_SCALE)
            expo[0, group, :top, lanes] = exponent
            max_hist[0, group, :, lanes] = new_max
            max_run[group, :, lanes] = new_max
            sum_run[group, :, lanes] = jnp.sum(exponent, axis=0, keepdims=True)
            out_acc[group, :, lanes] = matmul(value_t[0, :, :top], exponent.astype(BF16))

    def forward_next(j, group):
        scores = matmul(key_slots[j], q_t[group])
        old_max = max_run[group]
        new_max = jnp.maximum(old_max, jnp.max(scores, axis=0, keepdims=True))
        exponent = jnp.exp2((scores - new_max) * EXP2_SCALE)
        expo[j, group] = exponent
        max_hist[j, group] = new_max
        max_run[group] = new_max
        fade = jnp.exp2((old_max - new_max) * EXP2_SCALE)
        sum_run[group] = sum_run[group] * fade + jnp.sum(exponent, axis=0, keepdims=True)
        out_acc[group] = out_acc[group] * fade + matmul(value_t[j], exponent.astype(BF16))

    @pl.when(relay_in)
    def _():
        relay_copy(1).wait_recv()
        pass_copy(1).start()

    load_q.wait()

    def local_part(part, carry):
        for step in range(1, head_count):
            q_copy(step, part).wait_recv()
        for member in range(pair):
            group = part * pair + member
            piece = q_in[:, pl.ds(pl.multiple_of(group * HEAD_DIM, HEAD_DIM), HEAD_DIM)]
            q_rows[pl.ds(pl.multiple_of(group * BLOCK, BLOCK), BLOCK), :] = piece
            q_t[group] = piece.T
        for member in range(pair):
            forward_first(part * pair + member)
        for member in range(pair):
            forward_next(1, part * pair + member)
        return carry

    lax.fori_loop(0, HALVES, local_part, 0)

    def forward_slot(j, carry):
        @pl.when(s >= j - 1)
        def _():
            for kind in range(2):
                remote(
                    kv_send.at[j - 2, kind], slots[kind].at[j], kv_send_sem.at[j - 2, kind],
                    kv_recv_sem.at[j - 2, kind], (s, h)).wait_recv()
            transpose_slot(j)
            for group in range(groups):
                forward_next(j, group)
        return carry

    lax.fori_loop(2, SLOTS, forward_slot, 0)

    load_og.wait()
    for step in range(1, head_count):
        og_copy(step).wait_recv()

    for group in range(groups):
        lanes = slice(group * HEAD_DIM, (group + 1) * HEAD_DIM)
        piece = og_in[:, lanes]
        og_rows[group * BLOCK:(group + 1) * BLOCK, :] = piece
        piece_t = piece.T
        og_t[group] = piece_t
        inverse = 1.0 / sum_run[group]
        sum_run[group] = inverse
        attended = (out_acc[group] * inverse).astype(BF16)
        delta[group] = jnp.sum(piece_t.astype(F32) * attended.astype(F32), axis=0, keepdims=True)
        attn_send[:, lanes] = attended.T
        qgrad_acc[group] = jnp.zeros((HEAD_DIM, BLOCK), F32)

    def attn_copy(step):
        peer = lax.rem(h + step, head_count)
        return remote(
            attn_send.at[token_rows(peer), :], attn_recv.at[:, columns(h)],
            attn_send_sem.at[step], attn_recv_sem.at[step], (s, peer))

    def qgrad_copy(step, part):
        peer = lax.rem(h + step, head_count)
        return remote(
            qgrad_send.at[token_rows(peer), half_columns(0, part)], qgrad_recv.at[:, half_columns(h, part)],
            qgrad_send_sem.at[part, step], qgrad_recv_sem.at[part, step], (s, peer))

    def own_copy(source, target, sem):
        return pltpu.make_async_copy(source.at[token_rows(h), :], target.at[:, columns(h)], sem)

    for step in range(1, head_count):
        attn_copy(step).start()
    own_copy(attn_send, attn_recv, place_sem.at[0]).start()

    def grad_copy(j, kind):
        return remote(
            grad_send.at[j, kind], contrib.at[j, kind], grad_send_sem.at[j, kind], grad_recv_sem.at[j, kind],
            (s - (j - 1), h))

    def back_copy(kind):
        return remote(
            grad_send.at[2, kind], relay_grad.at[kind], back_send_sem.at[kind], back_recv_sem.at[kind],
            (s - RING, h))

    def pass_back(kind):
        return remote(
            relay_grad.at[kind], contrib.at[2, kind], pass_back_sem.at[kind], grad_recv_sem.at[2, kind],
            (s + (RING - 1), h))

    def grad_local(j):
        return pltpu.make_async_copy(grad_send.at[j], contrib.at[j], place_sem.at[2 + j])

    def backward_tile(j, group):
        factor = jnp.exp2((max_hist[j, group] - max_run[group]) * EXP2_SCALE) * sum_run[group]
        weights = expo[j, group] * factor
        weight_grad = matmul(value_slots[j], og_t[group])
        score_grad = (weights * (weight_grad - delta[group])).astype(BF16)
        qgrad_acc[group] += matmul(key_t[j], score_grad)
        return weights.astype(BF16), score_grad

    def backward_first(group):
        for top in (CORNER, BLOCK):
            lanes = slice(top - CORNER, top)
            factor = jnp.exp2((max_hist[0, group, :, lanes] - max_run[group, :, lanes]) * EXP2_SCALE)
            weights = expo[0, group, :top, lanes] * (factor * sum_run[group, :, lanes])
            weight_grad = matmul(value_slots[0, :top, :], og_t[group, :, lanes])
            score_grad = (weights * (weight_grad - delta[group, :, lanes])).astype(BF16)
            qgrad_acc[group, :, lanes] += matmul(key_t[0, :, :top], score_grad)
            place = pl.ds(pl.multiple_of(group * BLOCK + (top - CORNER), CORNER), CORNER)
            weights_low[0, :top, place] = weights.astype(BF16)
            scores_low[0, :top, place] = score_grad
            if top < BLOCK:
                weights_low[0, top:, place] = jnp.zeros((BLOCK - top, CORNER), BF16)
                scores_low[0, top:, place] = jnp.zeros((BLOCK - top, CORNER), BF16)

    def query_lanes(group):
        return slice(group * BLOCK, (group + 1) * BLOCK)

    def backward_slot(step, carry):
        j = SLOTS + 1 - step

        @pl.when(s >= j - 1)
        def _():
            for group in range(groups):
                weights, score_grad = backward_tile(j, group)
                weights_low[0, :, query_lanes(group)] = weights
                scores_low[0, :, query_lanes(group)] = score_grad
            grad_send[j, 0] = (matmul(scores_low[0], q_rows[...]) * SCALE).astype(BF16)
            grad_send[j, 1] = matmul(weights_low[0], og_rows[...]).astype(BF16)
            for kind in range(2):
                @pl.when(back_out & (j == 2))
                def _():
                    back_copy(kind).start()

                @pl.when(jnp.logical_not(back_out & (j == 2)))
                def _():
                    grad_copy(j, kind).start()
        return carry

    lax.fori_loop(2, SLOTS, backward_slot, 0)

    def local_back(part, carry):
        @pl.when(back_in)
        def _():
            for kind in range(2):
                @pl.when(part == min(kind, HALVES - 1))
                def _():
                    back_copy(kind).wait_recv()
                    pass_back(kind).start()
        for member in range(pair):
            backward_first(part * pair + member)
        for member in range(pair):
            group = part * pair + member
            weights, score_grad = backward_tile(1, group)
            lanes = pl.ds(pl.multiple_of(group * BLOCK, BLOCK), BLOCK)
            weights_low[1, :, lanes] = weights
            scores_low[1, :, lanes] = score_grad
        for member in range(pair):
            group = part * pair + member
            qgrad_send[:, pl.ds(pl.multiple_of(group * HEAD_DIM, HEAD_DIM), HEAD_DIM)] = (
                qgrad_acc[group] * SCALE).astype(BF16).T
        for step in range(1, head_count):
            qgrad_copy(step, part).start()
        return carry

    lax.fori_loop(0, HALVES, local_back, 0)
    own_copy(qgrad_send, qgrad_recv, place_sem.at[1]).start()
    for j in range(2):
        grad_send[j, 0] = (matmul(scores_low[j], q_rows[...]) * SCALE).astype(BF16)
        grad_send[j, 1] = matmul(weights_low[j], og_rows[...]).astype(BF16)
        grad_local(j).start()

    for step in range(1, head_count):
        og_copy(step).wait_send()
        attn_copy(step).wait()
        for part in range(HALVES):
            q_copy(step, part).wait_send()
    for distance in range(1, PICKS):
        @pl.when(s >= distance)
        def _():
            sel_copy(distance).wait_send()
    for kind in range(2):
        if kind == 1:
            @pl.when(relay_out)
            def _():
                relay_copy(kind).wait_send()

            @pl.when(relay_in)
            def _():
                pass_copy(kind).wait_send()

            @pl.when(jnp.logical_not(relay_out) & (s + 1 < seq_count))
            def _():
                kv_copy(1, kind).wait_send()
        else:
            @pl.when(s + 1 < seq_count)
            def _():
                kv_copy(1, kind).wait_send()

        @pl.when(back_out)
        def _():
            back_copy(kind).wait_send()

        @pl.when(jnp.logical_not(back_out) & (s >= 1))
        def _():
            grad_copy(2, kind).wait_send()

        @pl.when(back_in)
        def _():
            pass_back(kind).wait_send()

        for distance in range(2, PICKS):
            @pl.when(s + distance < seq_count)
            def _():
                kv_copy(distance, kind).wait_send()

            @pl.when(s >= distance)
            def _():
                grad_copy(distance + 1, kind).wait_send()
        for distance in range(1, PICKS):
            @pl.when(s + distance < seq_count)
            def _():
                grad_copy(distance + 1, kind).wait_recv()
    grad_local(0).wait()
    grad_local(1).wait()
    own_copy(attn_send, attn_recv, place_sem.at[0]).wait()
    own_copy(qgrad_send, qgrad_recv, place_sem.at[1]).wait()
    for part in range(HALVES):
        for step in range(1, head_count):
            qgrad_copy(step, part).wait()


def place_kernel(
    shard_blocks, target_ref, contrib, attn_in, qgrad_in,
    attn_out, qgrad_out, key_out, value_out,
    zeros, pieces, attn_buf, qgrad_buf, zero_sem, in_sem, out_sem, piece_in_sem, piece_out_sem,
):
    outs = (key_out, value_out)
    attn_load = pltpu.make_async_copy(attn_in, attn_buf, in_sem.at[0])
    qgrad_load = pltpu.make_async_copy(qgrad_in, qgrad_buf, in_sem.at[1])
    attn_load.start()
    qgrad_load.start()

    def piece_load(slot):
        return pltpu.make_async_copy(contrib.at[slot], pieces.at[slot], piece_in_sem.at[slot])

    targets = [target_ref[slot] for slot in range(SLOTS)]
    valid = [target >= 0 for target in targets]
    for slot in range(SLOTS):
        @pl.when(valid[slot])
        def _():
            piece_load(slot).start()

    zeros[...] = jnp.zeros_like(zeros)

    def taken(block):
        hit = targets[0] == block
        for slot in range(1, SLOTS):
            hit = hit | (targets[slot] == block)
        return hit

    def rows_of(block):
        return pl.ds(pl.multiple_of(block * BLOCK, BLOCK), BLOCK)

    def zero_copy(block, kind):
        return pltpu.make_async_copy(zeros, outs[kind].at[rows_of(block), :], zero_sem.at[kind, block])

    def zero_start(block, carry):
        @pl.when(jnp.logical_not(taken(block)))
        def _():
            zero_copy(block, 0).start()
            zero_copy(block, 1).start()
        return carry

    lax.fori_loop(0, shard_blocks, zero_start, 0)

    attn_store = pltpu.make_async_copy(attn_buf, attn_out, out_sem.at[0])
    qgrad_store = pltpu.make_async_copy(qgrad_buf, qgrad_out, out_sem.at[1])
    attn_load.wait()
    attn_store.start()
    qgrad_load.wait()
    qgrad_store.start()

    for slot in range(SLOTS):
        @pl.when(valid[slot])
        def _():
            piece_load(slot).wait()

    leads = []
    for slot in range(SLOTS):
        lead = valid[slot]
        for earlier in range(slot):
            lead = lead & jnp.logical_not(targets[earlier] == targets[slot])
        leads.append(lead)

    def piece_store(slot, kind):
        return pltpu.make_async_copy(
            pieces.at[slot, kind], outs[kind].at[rows_of(targets[slot]), :], piece_out_sem.at[slot, kind])

    for slot in range(SLOTS):
        @pl.when(leads[slot])
        def _():
            repeats = jnp.int32(0)
            for later in range(slot + 1, SLOTS):
                repeats = repeats + jnp.where(targets[later] == targets[slot], 1, 0)

            @pl.when(repeats > 0)
            def _():
                total = pieces[slot].astype(F32)
                for later in range(slot + 1, SLOTS):
                    total = total + jnp.where(targets[later] == targets[slot], pieces[later].astype(F32), 0.0)
                pieces[slot] = total.astype(BF16)
            piece_store(slot, 0).start()
            piece_store(slot, 1).start()

    def zero_wait(block, carry):
        @pl.when(jnp.logical_not(taken(block)))
        def _():
            zero_copy(block, 0).wait()
            zero_copy(block, 1).wait()
        return carry

    lax.fori_loop(0, shard_blocks, zero_wait, 0)
    for slot in range(SLOTS):
        @pl.when(leads[slot])
        def _():
            piece_store(slot, 0).wait()
            piece_store(slot, 1).wait()
    attn_store.wait()
    qgrad_store.wait()


def per_device(query, keys, values, out_grad, span_pos, selected):
    seq_count = lax.axis_size("seq")
    head_count = lax.axis_size("head")
    shard_blocks = keys.shape[0] // BLOCK
    rows, features = query.shape
    width = features // head_count
    groups = width // HEAD_DIM
    any_spec = pl.BlockSpec(memory_space=pl.ANY)
    smem_spec = pl.BlockSpec(memory_space=pltpu.SMEM)
    dma = pltpu.SemaphoreType.DMA
    contrib, attn_recv, qgrad_recv, targets = pl.pallas_call(
        functools.partial(attend_kernel, seq_count, head_count, groups, shard_blocks),
        out_shape=(
            jax.ShapeDtypeStruct((SLOTS, 2, BLOCK, HEAD_DIM), BF16),
            jax.ShapeDtypeStruct(query.shape, BF16),
            jax.ShapeDtypeStruct(query.shape, BF16),
            jax.ShapeDtypeStruct((8,), jnp.int32),
        ),
        in_specs=[smem_spec, smem_spec] + [any_spec] * 4,
        out_specs=(any_spec, any_spec, any_spec, smem_spec),
        scratch_shapes=[
            pltpu.SMEM((PICKS - 1, 1, PICKS), jnp.int32),
            pltpu.VMEM((shard_blocks, BLOCK, HEAD_DIM), BF16),
            pltpu.VMEM((shard_blocks, BLOCK, HEAD_DIM), BF16),
            pltpu.VMEM((BLOCK, width), BF16),
            pltpu.VMEM((BLOCK, width), BF16),
            pltpu.VMEM((groups * BLOCK, HEAD_DIM), BF16),
            pltpu.VMEM((groups * BLOCK, HEAD_DIM), BF16),
            pltpu.VMEM((groups, HEAD_DIM, BLOCK), BF16),
            pltpu.VMEM((groups, HEAD_DIM, BLOCK), BF16),
            pltpu.VMEM((SLOTS, BLOCK, HEAD_DIM), BF16),
            pltpu.VMEM((SLOTS, BLOCK, HEAD_DIM), BF16),
            pltpu.VMEM((SLOTS, HEAD_DIM, BLOCK), BF16),
            pltpu.VMEM((SLOTS, HEAD_DIM, BLOCK), BF16),
            pltpu.VMEM((PICKS - 1, 2, BLOCK, HEAD_DIM), BF16),
            pltpu.VMEM((SLOTS, 2, BLOCK, HEAD_DIM), BF16),
            pltpu.VMEM((2, BLOCK, HEAD_DIM), BF16),
            pltpu.VMEM((2, BLOCK, HEAD_DIM), BF16),
            pltpu.VMEM((SLOTS, groups, BLOCK, BLOCK), F32),
            pltpu.VMEM((SLOTS, groups, 1, BLOCK), F32),
            pltpu.VMEM((groups, 1, BLOCK), F32),
            pltpu.VMEM((groups, 1, BLOCK), F32),
            pltpu.VMEM((groups, 1, BLOCK), F32),
            pltpu.VMEM((groups, HEAD_DIM, BLOCK), F32),
            pltpu.VMEM((groups, HEAD_DIM, BLOCK), F32),
            pltpu.VMEM((2, BLOCK, groups * BLOCK), BF16),
            pltpu.VMEM((2, BLOCK, groups * BLOCK), BF16),
            pltpu.VMEM((BLOCK, width), BF16),
            pltpu.VMEM((BLOCK, width), BF16),
            dma((4,)),
            dma((PICKS - 1,)), dma((PICKS - 1,)),
            dma((HALVES, head_count)), dma((HALVES, head_count)),
            dma((head_count,)), dma((head_count,)),
            dma((PICKS - 1, 2)), dma((PICKS - 1, 2)),
            dma((2,)), dma((2,)), dma((2,)),
            dma((SLOTS, 2)), dma((SLOTS, 2)),
            dma((2,)), dma((2,)), dma((2,)),
            dma((head_count,)), dma((head_count,)),
            dma((HALVES, head_count)), dma((HALVES, head_count)),
            dma((4,)),
        ],
        compiler_params=pltpu.CompilerParams(
            collective_id=0, has_side_effects=True, vmem_limit_bytes=56 * 1024 * 1024),
        name="attend",
    )(selected, span_pos, query, out_grad,
      keys.reshape(shard_blocks, BLOCK, HEAD_DIM), values.reshape(shard_blocks, BLOCK, HEAD_DIM))

    return pl.pallas_call(
        functools.partial(place_kernel, shard_blocks),
        out_shape=(
            jax.ShapeDtypeStruct(query.shape, BF16),
            jax.ShapeDtypeStruct(query.shape, BF16),
            jax.ShapeDtypeStruct(keys.shape, BF16),
            jax.ShapeDtypeStruct(values.shape, BF16),
        ),
        in_specs=[smem_spec, any_spec, any_spec, any_spec],
        out_specs=(any_spec,) * 4,
        scratch_shapes=[
            pltpu.VMEM((BLOCK, HEAD_DIM), BF16),
            pltpu.VMEM((SLOTS, 2, BLOCK, HEAD_DIM), BF16),
            pltpu.VMEM(query.shape, BF16),
            pltpu.VMEM(query.shape, BF16),
            dma((2, shard_blocks)),
            dma((2,)),
            dma((2,)),
            dma((SLOTS,)),
            dma((SLOTS, 2)),
        ],
        name="place",
    )(targets, contrib, attn_recv, qgrad_recv)


def solution(mesh):
    in_specs = (
        P(("seq", "head"), None),
        P("seq", "head"),
        P("seq", "head"),
        P(("seq", "head"), None),
        P("seq"),
        P("seq", None),
    )
    out_specs = (
        P(("seq", "head"), None),
        P(("seq", "head"), None),
        P("seq", "head"),
        P("seq", "head"),
    )
    return jax.shard_map(
        per_device, mesh=mesh, in_specs=in_specs, out_specs=out_specs, check_vma=False
    )
```
